768 devices in a mesh: role: 2 (over y_hi), grp: 24 (over z, core), tp: 16 (over x, y_lo).
Axes of the slice: x: 4, y: 8 (y_hi: 2, y_lo: 4; y = y_hi * 4 + y_lo), z: 12, core: 2. Of those that a mesh axis runs over, the one named last changes fastest.
Arguments:
- learn_input: bfloat16 [98304, 8192], P(('role', 'grp', 'tp')), may hold values from -6 to 6
- grad_output: bfloat16 [98304, 8192], P(('role', 'grp', 'tp')), may hold values from -6 to 6
- factor_down: bfloat16 [64, 8192], P(None, 'tp'), may hold values from -4 to 4
- factor_up: bfloat16 [64, 8192], P(None, 'tp'), may hold values from -4 to 4
- layer_scales: float32 [80, 64], replicated, may hold values from -4 to 4
- layer_index: int32 [1], replicated, may hold values from 0 to 79
- decode_input: bfloat16 [48, 8192], P(('role', 'grp')), may hold values from -6 to 6
- base_query: bfloat16 [48, 8192], P(('role', 'grp')), may hold values from -5 to 5
- key_cache: bfloat16 [48, 1024, 1024], P(('role', 'grp'), 'tp'), may hold values from -5 to 5
- value_cache: bfloat16 [48, 1024, 1024], P(('role', 'grp'), 'tp'), may hold values from -6 to 6
- fresh_key: bfloat16 [48, 1024], P(('role', 'grp')), may hold values from -6 to 6
- fresh_value: bfloat16 [48, 1024], P(('role', 'grp')), may hold values from -6 to 6
- cache_lengths: int32 [48], P(('role', 'grp')), may hold values from 1 to 1024, 24576 in all
Outputs:
- updated_down: bfloat16 [64, 8192], P(None, 'tp')
- updated_up: bfloat16 [64, 8192], P(None, 'tp')
- updated_scales: float32 [64], replicated
- attended: bfloat16 [48, 8192], P(('role', 'grp'))
The draws below stay inside these ranges and needn't reach their ends.
Inputs may be any that keep to these rules, and one draw needn't show every extreme that they name: `cache_lengths`: some row has exactly 1024 live positions.
All inputs are finite; a program needn't handle non-finite values. No bound on the sum of `cache_lengths` on one device may be relied on, other than what follows from the above.
Results may differ from the reference program's by a relative error of at most 0.013.
Values may be sent and summed in bfloat16 or wider, within the bound.
A program may use at most 32 MiB of HBM per device.

```python
import math
import jax
import jax.numpy as jnp
import numpy as np
from jax import lax

D = 8192
HEADS = 64
KVH = 8
HD = 128
R = 64
LAYERS = 80
CACHE = 1024
QW = 8192
KVW = 1024
TOKENS = 98304
ROWS = 48


def draw_base_query(key, part):
    drawn = jnp.clip(jax.random.normal(jax.random.fold_in(key, 1), (ROWS, QW), jnp.float32), -4.0, 4.0)
    return drawn.astype(jnp.bfloat16)


def draw_key_cache(key, part):
    drawn = jnp.clip(jax.random.normal(jax.random.fold_in(key, 2), (ROWS, CACHE, KVW), jnp.float32), -4.0, 4.0)
    return drawn.astype(jnp.bfloat16)


def level_of(key, dims, shards, low, high):
    loudness = 1.0
    for dim, blocks in shards:
        heights = jax.random.uniform(jax.random.fold_in(jax.random.fold_in(key, 6), dim), (blocks,), jnp.float32, low / len(shards), high / len(shards))
        loudness = loudness * jnp.repeat(jnp.exp(heights), dims[dim] // blocks).reshape((-1,) + (1,) * (len(dims) - 1 - dim))
    return loudness


def length_profile(amount, total, limit, lean):
    loads = [(1 << 20) // math.isqrt(grade ** lean) + 1 for grade in range(2, amount + 1)]
    rest, given = total - limit - (amount - 1), [1] * (amount - 1)
    while rest > 0:
        candidates = [i for i in range(amount - 1) if given[i] < limit]
        pool, budget = sum([loads[i] for i in candidates]), rest
        for i in candidates:
            more = min(limit - given[i], max(1, budget * loads[i] // pool), rest)
            given[i] = given[i] + more
            rest = rest - more
    return np.array([limit] + given)


def ragged_sizes(rng, count, total, bound, skew):
    if count == 2:
        one = jax.random.randint(rng, (), max(1, total - bound), min(bound, total - 1) + 1)
        return jnp.stack([one, total - one])
    tallies = jnp.asarray(length_profile(count, total, bound, skew), jnp.int32)
    pairs = (count - 1) // 2
    donor, receiver = tallies[1:1 + 2 * pairs:2], tallies[2:2 + 2 * pairs:2]
    room = jnp.minimum(donor - 1, bound - receiver)
    passed = jax.random.randint(jax.random.fold_in(rng, 1), (pairs,), 0, 1 << 20) % (room + 1)
    tallies = tallies.at[1:1 + 2 * pairs:2].set(donor - passed).at[2:2 + 2 * pairs:2].set(receiver + passed)
    return tallies[jax.random.permutation(jax.random.fold_in(rng, 2), count)]


def scatter_about(stream_key, shape, deviation, bound, cuts=(), kind=jnp.bfloat16):
    values = deviation * jax.random.normal(stream_key, shape, jnp.float32)
    if cuts:
        values = values * level_of(stream_key, shape, cuts, -0.22, 0.18)
    return jnp.clip(values, -bound, bound).astype(kind)


def setup_inputs(seed: int = 0) -> dict:
    splits = jax.random.split(jax.random.key(seed), 14)
    return {
        "learn_input": scatter_about(splits[0], (TOKENS, D), 1.0, 6.0, ((0, 768),)),
        "grad_output": scatter_about(splits[1], (TOKENS, QW), 1.0, 6.0, ((0, 768),)),
        "factor_down": scatter_about(splits[2], (R, D), 0.25, 4.0, ((1, 16),)),
        "factor_up": scatter_about(splits[3], (R, QW), 0.25, 4.0, ((1, 16),)),
        "layer_scales": scatter_about(splits[4], (LAYERS, R), 1.0, 4.0, (), jnp.float32),
        "layer_index": jax.random.randint(splits[5], (1,), 0, LAYERS).astype(jnp.int32),
        "decode_input": scatter_about(splits[6], (ROWS, D), 1.0, 6.0, ((0, 48),)),
        "base_query": draw_base_query(jax.random.fold_in(splits[13], 71), 0),
        "key_cache": draw_key_cache(jax.random.fold_in(splits[13], 71), 0),
        "value_cache": scatter_about(splits[9], (ROWS, CACHE, KVW), 0.5, 6.0, ((0, 48), (1, 16))),
        "fresh_key": scatter_about(splits[10], (ROWS, KVW), 1.0, 6.0, ((0, 48),)),
        "fresh_value": scatter_about(splits[11], (ROWS, KVW), 0.5, 6.0, ((0, 48),)),
        "cache_lengths": ragged_sizes(splits[12], ROWS, ROWS * CACHE // 2, CACHE, 0).astype(jnp.int32),
    }


rate_down = 8.0
rate_up = 8.0
rate_scale = 0.1

def attend_row(inputs):
    query_row, key_rows, value_rows, fresh_key_row, fresh_value_row, length = inputs
    groups = HEADS // KVH
    key_scale = 1.0 / math.sqrt(HD)
    high = lax.Precision.HIGHEST
    query_heads = query_row.astype(jnp.float32).reshape(KVH, groups, HD)
    key_heads = key_rows.astype(jnp.float32).reshape(CACHE, KVH, HD)
    value_heads = value_rows.astype(jnp.float32).reshape(CACHE, KVH, HD)
    scores = jnp.einsum('kgd,pkd->kgp', query_heads, key_heads, precision=high) * key_scale
    live_mask = jnp.arange(CACHE, dtype=jnp.int32) < length
    fresh_score = jnp.einsum('kgd,kd->kg', query_heads, fresh_key_row.astype(jnp.float32).reshape(KVH, HD), precision=high) * key_scale
    highest = jnp.maximum(lax.optimization_barrier(jnp.max(jnp.where(live_mask, scores, -1e+30), axis=2)), fresh_score)
    weights = jnp.where(live_mask, jnp.exp(scores - highest[:, :, None]), 0.0)
    fresh_weight = jnp.exp(fresh_score - highest)
    denominator = lax.optimization_barrier(jnp.sum(weights, axis=2)) + fresh_weight
    rounded = lax.optimization_barrier(weights.astype(jnp.bfloat16)).astype(jnp.float32)
    numerator = jnp.einsum('kgp,pkd->kgd', rounded, value_heads, precision=high)
    fresh_rounded = lax.optimization_barrier(fresh_weight.astype(jnp.bfloat16)).astype(jnp.float32)
    numerator = numerator + fresh_rounded[:, :, None] * fresh_value_row.astype(jnp.float32).reshape(KVH, 1, HD)
    return (numerator / denominator[:, :, None]).reshape(HEADS * HD).astype(jnp.bfloat16)

def reference(learn_input, grad_output, factor_down, factor_up, layer_scales, layer_index, decode_input, base_query, key_cache, value_cache, fresh_key, fresh_value, cache_lengths):
    layer_scale = lax.dynamic_slice_in_dim(layer_scales, layer_index[0].astype(jnp.int32), 1, 0)[0]
    scale_down = 1.0 / math.sqrt(D)
    scale_up = 1.0 / math.sqrt(R)
    contract_rank = (((1,), (1,)), ((), ()))
    contract_tokens = (((0,), (0,)), ((), ()))
    hidden = lax.dot_general(learn_input, factor_down, contract_rank, preferred_element_type=jnp.float32) * scale_down
    back_signal = lax.dot_general(grad_output, factor_up, contract_rank, preferred_element_type=jnp.float32) * scale_up
    scaled = (hidden * layer_scale).astype(jnp.bfloat16)
    back_scaled = (back_signal * layer_scale).astype(jnp.bfloat16)
    gradient_down = lax.dot_general(back_scaled, learn_input, contract_tokens, preferred_element_type=jnp.float32) * scale_down
    gradient_up = lax.dot_general(scaled, grad_output, contract_tokens, preferred_element_type=jnp.float32) * scale_up
    gradient_scale = lax.optimization_barrier(jnp.sum(hidden * back_signal, axis=0))
    step_scale = 1.0 / math.sqrt(TOKENS)
    updated_down = (factor_down.astype(jnp.float32) - rate_down * step_scale * gradient_down).astype(jnp.bfloat16)
    updated_up = (factor_up.astype(jnp.float32) - rate_up * step_scale * gradient_up).astype(jnp.bfloat16)
    updated_scales = layer_scale - rate_scale * step_scale * gradient_scale
    decode_hidden = lax.dot_general(decode_input, updated_down, contract_rank, preferred_element_type=jnp.float32) * scale_down
    decode_scaled = (decode_hidden * updated_scales).astype(jnp.bfloat16)
    query_rows = (base_query.astype(jnp.float32) + jnp.dot(decode_scaled, updated_up, preferred_element_type=jnp.float32) * scale_up).astype(jnp.bfloat16)
    attended = lax.map(attend_row, (query_rows, key_cache, value_cache, fresh_key, fresh_value, cache_lengths))
    return (updated_down, updated_up, updated_scales, attended)
```

```python
import math

import jax
import jax.numpy as jnp
from jax import lax
from jax.experimental import pallas as pl
from jax.experimental.pallas import tpu as pltpu
from jax.sharding import PartitionSpec as P

HEADS = 64
KVH = 8
HD = 128

rate_down = 8.0
rate_up = 8.0
rate_scale = 0.1

MESH = pl.DeviceIdType.MESH
NX = 4
NY = 4
ZL = 4
F32 = jnp.float32
BF16 = jnp.bfloat16


def kernel(
    roles, grps, tps,
    learn, grad, fdown, fup, lscales, lindex, dinput, bquery, kcache, vcache, fkey, fvalue, lengths,
    ndown, nup, nscale, att,
    xbuf, fall, sx, gbuf, rc, rs_src, rs_dst, z_src, z_dst, fown, nb, dh, kv_src, kv, atb, ls, din, bq, fk, fv,
    loc, xs, xr, fs, fr, ss, sr, gs, gr, ks, kr, r3s, r3r, r4s, r4r, n5s, n5r, dhs, dhr, ats, atr,
):
    cols = fdown.shape[1]
    rank = fdown.shape[0]
    toks = learn.shape[0]
    width = learn.shape[1]
    zh_n = grps // (2 * ZL)
    role = lax.axis_index("role")
    grp = lax.axis_index("grp")
    tp = lax.axis_index("tp")
    x, ylo = tp // NY, tp % NY
    y = role * NY + ylo
    z, core = grp // 2, grp % 2
    zh, zl = z // ZL, z % ZL
    ny = roles * NY
    other = 1 - core
    sib = (role, z * 2 + other, tp)

    def plane(dx, dy, sign):
        d = dy - NY if dy == NY - 1 else dy
        xx = (x + sign * dx + NX) % NX
        yy = (y + sign * d + ny) % ny
        return (yy // NY, grp, xx * NY + yy % NY)

    offsets = [(dx, dy) for dx in range(NX) for dy in range(NY) if dx or dy]
    n_plane = len(offsets)

    def team(d):
        b = (role * ZL + zl + d) % (roles * ZL)
        return b // ZL, zh * ZL + b % ZL

    block = role * ZL + zl
    n_team = roles * ZL

    def far(e):
        return (role, (((zh + e) % zh_n) * ZL + zl) * 2 + core, tp)

    local = []

    def fetch(src, dst):
        c = pltpu.make_async_copy(src, dst, loc.at[len(local)])
        c.start()
        local.append(c)
        return c

    sends = []

    def send(src, dst, s, r, dev):
        c = pltpu.make_async_remote_copy(
            src_ref=src, dst_ref=dst, send_sem=s, recv_sem=r, device_id=dev, device_id_type=MESH
        )
        c.start()
        sends.append(c)
        return c

    @pl.when(core == 0)
    def _():
        pltpu.make_async_copy(fdown, fall.at[tp], loc.at[0]).start()
        pltpu.make_async_copy(learn, xbuf.at[core], loc.at[1]).start()

    @pl.when(core == 1)
    def _():
        pltpu.make_async_copy(fup, fall.at[tp], loc.at[0]).start()
        pltpu.make_async_copy(grad, xbuf.at[core], loc.at[1]).start()

    c_f = pltpu.make_async_copy(fdown, fall.at[tp], loc.at[0])
    c_x = pltpu.make_async_copy(learn, xbuf.at[core], loc.at[1])
    local.extend([c_f, c_x])
    c_ls = fetch(lscales, ls)
    c_din = fetch(dinput, din)
    c_bq = fetch(bquery, bq)
    c_fk = fetch(fkey, fk)
    c_fv = fetch(fvalue, fv)
    c_k = fetch(kcache.at[0], kv_src.at[0])
    c_v = fetch(vcache.at[0], kv_src.at[1])

    with jax.named_scope("greet"):
        barrier = pltpu.get_barrier_semaphore()

        def greet(dev):
            pl.semaphore_signal(barrier, inc=1, device_id=dev, device_id_type=MESH)

        for dx, dy in offsets:
            greet(plane(dx, dy, -1))
        for d in range(1, tps):
            greet((role, grp, (tp + d) % tps))
        greet(sib)
        for d in range(1, n_team):
            rr, zz = team(d)
            greet((rr, zz * 2 + core, tp))
            greet((rr, zz * 2 + other, tp))
        for e in range(1, zh_n):
            greet(far(e))
        pl.semaphore_wait(barrier, n_plane + tps - 1 + 1 + 2 * (n_team - 1) + zh_n - 1)

    with jax.named_scope("send_own"):
        @pl.when(core == 0)
        def _():
            pltpu.make_async_remote_copy(
                src_ref=grad, dst_ref=xbuf.at[core], send_sem=xs.at[0], recv_sem=xr.at[0],
                device_id=sib, device_id_type=MESH,
            ).start()

        @pl.when(core == 1)
        def _():
            pltpu.make_async_remote_copy(
                src_ref=learn, dst_ref=xbuf.at[core], send_sem=xs.at[0], recv_sem=xr.at[0],
                device_id=sib, device_id_type=MESH,
            ).start()

        c_xs = pltpu.make_async_remote_copy(
            src_ref=learn, dst_ref=xbuf.at[core], send_sem=xs.at[0], recv_sem=xr.at[0],
            device_id=sib, device_id_type=MESH,
        )
        c_f.wait()
        gathers = []
        for i, (dx, dy) in enumerate(offsets):
            gathers.append(send(fall.at[tp], fall.at[tp], fs.at[i], fr.at[i], plane(dx, dy, 1)))

    sc = jnp.where(core == 0, 1.0 / math.sqrt(width), 1.0 / math.sqrt(rank)).astype(F32)
    rate = jnp.where(core == 0, rate_down, rate_up).astype(F32)
    step_scale = 1.0 / math.sqrt(toks * roles * grps * tps)
    fown[...] = fall[tp].astype(F32).reshape(fown.shape)

    c_ls.wait()
    row_i = lax.broadcasted_iota(jnp.int32, ls.shape, 0)
    ls_row = jnp.sum(jnp.where(row_i == lindex[0], ls[...], 0.0), axis=0, keepdims=True)
    eye = lax.broadcasted_iota(jnp.int32, (rank, rank), 0) == lax.broadcasted_iota(jnp.int32, (rank, rank), 1)

    def to_col(row):
        return jnp.sum(jnp.where(eye, jnp.broadcast_to(row, (rank, rank)), 0.0), axis=1, keepdims=True)

    def to_row(col):
        return jnp.sum(jnp.where(eye, jnp.broadcast_to(col, (rank, rank)), 0.0), axis=0, keepdims=True)

    ls_col = to_col(ls_row)

    def operand(slot):
        return xbuf[:, :, pl.ds(pl.multiple_of(slot * cols, cols), cols)].reshape(2 * toks, cols)

    NT = (((1,), (1,)), ((), ()))
    with jax.named_scope("project"):
        c_x.wait()
        c_xs.wait_recv()
        acc = lax.dot_general(fall[tp], operand(tp), NT, preferred_element_type=F32)
        for i, (dx, dy) in enumerate(offsets):
            gathers[i].wait_recv()
            slot = ((x - dx + NX) % NX) * NY + (ylo - dy + NY) % NY
            acc = acc + lax.dot_general(fall[slot], operand(slot), NT, preferred_element_type=F32)
        sx[core] = acc * sc

    with jax.named_scope("swap_projection"):
        c_s = send(sx.at[core], sx.at[core], ss.at[0], sr.at[0], sib)
        c_s.wait_recv()

    with jax.named_scope("gradient"):
        term = (sx[other] * ls_col).astype(BF16)
        scatters = []
        for i, (dx, dy) in enumerate(offsets):
            dev = plane(dx, dy, 1)
            slot = dev[2]
            g = jnp.dot(term, operand(slot), preferred_element_type=F32) * sc
            gbuf[slot] = g.astype(BF16)
            scatters.append(send(gbuf.at[slot], rc.at[i], gs.at[i], gr.at[i], dev))
        total = jnp.dot(term, operand(tp), preferred_element_type=F32) * sc
        scale_row = to_row(jnp.sum(sx[0] * sx[1], axis=1, keepdims=True))

    with jax.named_scope("send_cache"):
        c_k.wait()
        c_v.wait()
        caches = []
        head = tp // 2
        kv[:, tp] = kv_src[:, :, pl.ds(pl.multiple_of(head * HD, HD), HD)]
        for d in range(1, tps):
            to = (tp + d) % tps
            his = pl.ds(pl.multiple_of((to // 2) * HD, HD), HD)
            caches.append(
                send(kv_src.at[:, :, his], kv.at[:, tp], ks.at[d - 1], kr.at[d - 1], (role, grp, to))
            )

    with jax.named_scope("sum_plane"):
        for i in range(n_plane):
            scatters[i].wait_recv()
            total = total + rc[i].astype(F32)
        rs_src[:, :, :cols] = total.reshape(n_team, rank // n_team, cols)
        wide = jnp.concatenate([scale_row, jnp.zeros_like(scale_row)], axis=1)
        rs_src[:, :, cols:] = jnp.broadcast_to(wide, (n_team, rank // n_team, 2 * rank))

    with jax.named_scope("sum_team"):
        team_c = []
        for d in range(1, n_team):
            rr, zz = team(d)
            b = (block + d) % n_team
            team_c.append(
                send(rs_src.at[b], rs_dst.at[d - 1], r3s.at[d - 1], r3r.at[d - 1], (rr, zz * 2 + core, tp))
            )
        part = rs_src[block]
        for d in range(1, n_team):
            team_c[d - 1].wait_recv()
            part = part + rs_dst[d - 1]

    with jax.named_scope("sum_far"):
        z_src[...] = part
        far_c = []
        for e in range(1, zh_n):
            far_c.append(send(z_src, z_dst.at[e - 1], r4s.at[e - 1], r4r.at[e - 1], far(e)))
        for e in range(1, zh_n):
            far_c[e - 1].wait_recv()
            part = part + z_dst[e - 1]

    with jax.named_scope("spread_factors"):
        new = fown[block] - (rate * step_scale) * part[:, :cols]
        nb[core, block] = new.astype(BF16).astype(F32)
        spread = []
        mine = nb.at[core, block]
        spread.append(send(mine, mine, n5s.at[0, 0], n5r.at[0, 0], sib))
        for d in range(1, n_team):
            rr, zz = team(d)
            spread.append(send(mine, mine, n5s.at[0, d], n5r.at[0, d], (rr, zz * 2 + core, tp)))
            spread.append(send(mine, mine, n5s.at[1, d], n5r.at[1, d], (rr, zz * 2 + other, tp)))
        c_din.wait()
        drow = jnp.broadcast_to(
            din[:, pl.ds(pl.multiple_of(tp * cols, cols), cols)].astype(F32), (16, cols)
        ).astype(BF16)
        for c in spread:
            c.wait_recv()
        new_down = nb[0].reshape(rank, cols).astype(BF16)
        new_up = nb[1].reshape(rank, cols).astype(BF16)
        ndown[...] = new_down
        nup[...] = new_up

    with jax.named_scope("decode_hidden"):
        hid = lax.dot_general(drow, new_down, NT, preferred_element_type=F32)[:1]
        dh[tp] = jnp.concatenate([hid, part[:1, cols:cols + rank]], axis=1)
        hid_c = []
        for d in range(1, tps):
            hid_c.append(send(dh.at[tp], dh.at[tp], dhs.at[d - 1], dhr.at[d - 1], (role, grp, (tp + d) % tps)))
        for c in hid_c:
            c.wait_recv()
        both = jnp.sum(dh[...], axis=0)
        scale_total = pltpu.roll(both, rank, 1)[:, :rank]
        new_scales = ls_row - (rate_scale * step_scale) * scale_total
        nscale[...] = new_scales
        dscaled = (both[:, :rank] * (1.0 / math.sqrt(width)) * new_scales)
        dscaled = jnp.broadcast_to(dscaled, (16, rank)).astype(BF16)
        c_bq.wait()
        q = jnp.dot(dscaled, new_up, preferred_element_type=F32)[:1] * (1.0 / math.sqrt(rank))
        q = bq[:, pl.ds(pl.multiple_of(tp * cols, cols), cols)].astype(F32) + q
        mine_n = cols // HD
        q = jnp.concatenate([q[:, h * HD:(h + 1) * HD] for h in range(mine_n)] + [jnp.zeros((16 - mine_n, HD), F32)], axis=0).astype(BF16)

    with jax.named_scope("attend"):
        c_fk.wait()
        c_fv.wait()
        for c in caches:
            c.wait_recv()
        hs = pl.ds(pl.multiple_of(head * HD, HD), HD)
        n_pos = tps * kv.shape[2]
        keys = kv[0].reshape(n_pos, HD)
        values = kv[1].reshape(n_pos, HD)
        key_scale = 1.0 / math.sqrt(HD)
        s = lax.dot_general(q, keys, NT, preferred_element_type=F32) * key_scale
        fresh = jnp.sum(q.astype(F32) * fk[:, hs].astype(F32), axis=1, keepdims=True) * key_scale
        live = lax.broadcasted_iota(jnp.int32, s.shape, 1) < lengths[0]
        high = jnp.maximum(jnp.max(jnp.where(live, s, -1e30), axis=1, keepdims=True), fresh)
        w = jnp.where(live, jnp.exp(s - high), 0.0)
        fw = jnp.exp(fresh - high)
        den = jnp.sum(w, axis=1, keepdims=True) + fw
        num = jnp.dot(w.astype(BF16), values, preferred_element_type=F32)
        num = num + fw.astype(BF16).astype(F32) * fv[:, hs].astype(F32)
        res = num / den
        atb[tp] = res[:mine_n]

    with jax.named_scope("spread_attended"):
        at_c = []
        for d in range(1, tps):
            at_c.append(send(atb.at[tp], atb.at[tp], ats.at[d - 1], atr.at[d - 1], (role, grp, (tp + d) % tps)))
        for c in at_c:
            c.wait_recv()
        for s_ in range(tps):
            att[s_ * mine_n:(s_ + 1) * mine_n, :] = atb[s_]

    with jax.named_scope("drain"):
        c_xs.wait_send()
        for c in sends:
            c.wait_send()


def body(*args):
    learn, grad, fdown = args[0], args[1], args[2]
    roles, grps, tps = (lax.axis_size(a) for a in ("role", "grp", "tp"))
    rank, cols = fdown.shape
    toks, width = learn.shape
    local_pos = args[8].shape[1]
    n_plane = NX * NY - 1
    n_team = roles * ZL
    zh_n = grps // (2 * ZL)
    mine_n = cols // HD
    kvw = args[10].shape[1]
    any_spec = pl.BlockSpec(memory_space=pl.ANY)
    smem = pl.BlockSpec(memory_space=pltpu.SMEM)
    vmem = pl.BlockSpec(memory_space=pltpu.VMEM)
    in_specs = [any_spec] * 5 + [smem] + [any_spec] * 6 + [smem]
    rb = rank // n_team
    dma = pltpu.SemaphoreType.DMA
    outs = pl.pallas_call(
        lambda *refs: kernel(roles, grps, tps, *refs),
        out_shape=(
            jax.ShapeDtypeStruct((rank, cols), BF16),
            jax.ShapeDtypeStruct((rank, cols), BF16),
            jax.ShapeDtypeStruct((1, rank), F32),
            jax.ShapeDtypeStruct((HEADS, HD), F32),
        ),
        in_specs=in_specs,
        out_specs=(vmem, vmem, vmem, vmem),
        scratch_shapes=[
            pltpu.VMEM((2, toks, width), BF16),
            pltpu.VMEM((tps, rank, cols), BF16),
            pltpu.VMEM((2, rank, 2 * toks), F32),
            pltpu.VMEM((tps, rank, cols), BF16),
            pltpu.VMEM((n_plane, rank, cols), BF16),
            pltpu.VMEM((n_team, rb, cols + 2 * rank), F32),
            pltpu.VMEM((n_team - 1, rb, cols + 2 * rank), F32),
            pltpu.VMEM((rb, cols + 2 * rank), F32),
            pltpu.VMEM((zh_n - 1, rb, cols + 2 * rank), F32),
            pltpu.VMEM((n_team, rb, cols), F32),
            pltpu.VMEM((2, n_team, rb, cols), F32),
            pltpu.VMEM((tps, 1, 2 * rank), F32),
            pltpu.VMEM((2, local_pos, kvw), BF16),
            pltpu.VMEM((2, tps, local_pos, HD), BF16),
            pltpu.VMEM((tps, mine_n, HD), F32),
            pltpu.VMEM(args[4].shape, F32),
            pltpu.VMEM((1, width), BF16),
            pltpu.VMEM((1, width), BF16),
            pltpu.VMEM((1, kvw), BF16),
            pltpu.VMEM((1, kvw), BF16),
            dma((9,)),
            dma((1,)), dma((1,)),
            dma((n_plane,)), dma((n_plane,)),
            dma((1,)), dma((1,)),
            dma((n_plane,)), dma((n_plane,)),
            dma((tps - 1,)), dma((tps - 1,)),
            dma((n_team - 1,)), dma((n_team - 1,)),
            dma((zh_n - 1,)), dma((zh_n - 1,)),
            dma((2, n_team)), dma((2, n_team)),
            dma((tps - 1,)), dma((tps - 1,)),
            dma((tps - 1,)), dma((tps - 1,)),
        ],
        compiler_params=pltpu.CompilerParams(
            collective_id=0, has_side_effects=True, vmem_limit_bytes=48 * 1024 * 1024
        ),
    )(*args)
    return (
        outs[0],
        outs[1],
        outs[2].reshape(rank),
        outs[3].astype(BF16).reshape(1, HEADS * HD),
    )


def solution(mesh):
    in_specs = (
        P(("role", "grp", "tp"), None),
        P(("role", "grp", "tp"), None),
        P(None, "tp"),
        P(None, "tp"),
        P(),
        P(),
        P(("role", "grp"), None),
        P(("role", "grp"), None),
        P(("role", "grp"), "tp", None),
        P(("role", "grp"), "tp", None),
        P(("role", "grp"), None),
        P(("role", "grp"), None),
        P(("role", "grp")),
    )
    out_specs = (P(None, "tp"), P(None, "tp"), P(), P(("role", "grp"), None))
    return jax.shard_map(body, mesh=mesh, in_specs=in_specs, out_specs=out_specs, check_vma=False)
```

```python
import math

import jax
import jax.numpy as jnp
from jax import lax
from jax.experimental import pallas as pl
from jax.experimental.pallas import tpu as pltpu
from jax.sharding import PartitionSpec as P

HEADS = 64
KVH = 8
HD = 128

rate_down = 8.0
rate_up = 8.0
rate_scale = 0.1

MESH = pl.DeviceIdType.MESH
NX = 4
NY = 4
ZL = 4
F32 = jnp.float32
BF16 = jnp.bfloat16


def kernel(
    roles, grps, tps,
    learn, grad, fdown, fup, lscales, lindex, dinput, bquery, kcache, vcache, fkey, fvalue, lengths,
    ndown, nup, nscale, att,
    xbuf, fall, sx, gbuf, rx, ry, p_src, ry2, rx2, rs_src, rs_dst, z_src, z_dst, nb, dh, kv_src, kv, atb, ls, din, bq, fk, fv,
    loc, xs, xr, a1s, a1r, a2s, a2r, ss, sr, c1s, c1r, c2s, c2r, ks, kr, r3s, r3r, r4s, r4r, n5s, n5r, dhs, dhr, ats, atr, oc,
):
    rank, cols = fdown.shape
    toks, width = learn.shape
    zn = grps // 2
    half = rank // 2
    quart = rank // 4
    role = lax.axis_index("role")
    grp = lax.axis_index("grp")
    tp = lax.axis_index("tp")
    x, ylo = tp // NY, tp % NY
    y = role * NY + ylo
    z, core = grp // 2, grp % 2
    ny = roles * NY
    other = 1 - core
    sib = (role, z * 2 + other, tp)

    XS = tuple(range(1, NX))

    def at_x(dx):
        return (role, grp, (x + dx + NX) % NX * NY + ylo)

    def at_y(dy):
        yy = (y + dy + ny) % ny
        return (yy // NY, grp, x * NY + yy % NY)

    def xi(dx):
        return (x + dx + NX) % NX

    def yi(dy):
        return (ylo + dy + NY) % NY

    def at_z(dz, c, dr=0):
        return ((role + dr) % roles, (z + dz + zn) % zn * 2 + c, tp)

    local = []

    def fetch(src, dst):
        c = pltpu.make_async_copy(src, dst, loc.at[len(local)])
        c.start()
        local.append(c)
        return c

    sends = []

    def copy(src, dst, s, r, dev):
        return pltpu.make_async_remote_copy(
            src_ref=src, dst_ref=dst, send_sem=s, recv_sem=r, device_id=dev, device_id_type=MESH
        )

    def send(src, dst, s, r, dev):
        c = copy(src, dst, s, r, dev)
        c.start()
        sends.append(c)
        return c

    @pl.when(core == 0)
    def _():
        pltpu.make_async_copy(fdown, fall.at[x, ylo], loc.at[0]).start()
        pltpu.make_async_copy(learn, xbuf.at[core], loc.at[1]).start()

    @pl.when(core == 1)
    def _():
        pltpu.make_async_copy(fup, fall.at[x, ylo], loc.at[0]).start()
        pltpu.make_async_copy(grad, xbuf.at[core], loc.at[1]).start()

    c_f = pltpu.make_async_copy(fdown, fall.at[x, ylo], loc.at[0])
    c_x = pltpu.make_async_copy(learn, xbuf.at[core], loc.at[1])
    local.extend([c_f, c_x])
    c_k = fetch(kcache.at[0], kv_src.at[0])
    c_v = fetch(vcache.at[0], kv_src.at[1])
    c_ls = fetch(lscales, ls)
    c_din = fetch(dinput, din)
    c_bq = fetch(bquery, bq)
    c_fk = fetch(fkey, fk)
    c_fv = fetch(fvalue, fv)

    FAR = tuple(range(ZL, zn, ZL))
    NEAR = (1, -1, 2)
    TEAM = [(dz, dr) for dr in range(roles) for dz in (0,) + NEAR if dz or dr]

    with jax.named_scope("greet"):
        barrier = pltpu.get_barrier_semaphore()

        def greet(dev):
            pl.semaphore_signal(barrier, inc=1, device_id=dev, device_id_type=MESH)

        greet(sib)
        for dy in (1, -1, 2, -2):
            greet(at_y(dy))
        for d in range(1, tps):
            greet((role, grp, (tp + d) % tps))
        for dz, dr in TEAM:
            greet(at_z(-dz, core, dr))
        for dz in NEAR:
            greet(at_z(-dz, other))
        for dz in FAR:
            greet(at_z(-dz, core))
        pl.semaphore_wait(barrier, 1 + 4 + tps - 1 + len(TEAM) + len(NEAR) + len(FAR))

    with jax.named_scope("send_own"):
        @pl.when(core == 0)
        def _():
            copy(grad, xbuf.at[core], xs.at[0], xr.at[0], sib).start()

        @pl.when(core == 1)
        def _():
            copy(learn, xbuf.at[core], xs.at[0], xr.at[0], sib).start()

        c_xs = copy(learn, xbuf.at[core], xs.at[0], xr.at[0], sib)
        c_f.wait()
        lo, hi = pl.ds(0, half), pl.ds(half, half)
        own = fall.at[x, ylo]
        ax = {dx: send(own, own, a1s.at[dx - 1], a1r.at[dx - 1], at_x(dx)) for dx in XS}
        ay = {
            1: [send(own, own, a1s.at[3], a1r.at[3], at_y(1))],
            -1: [send(own, own, a1s.at[4], a1r.at[4], at_y(-1))],
        }
        ay[2] = [
            send(fall.at[x, ylo, lo], fall.at[x, ylo, lo], a1s.at[5], a1r.at[5], at_y(2)),
            send(fall.at[x, ylo, hi], fall.at[x, ylo, hi], a1s.at[6], a1r.at[6], at_y(-2)),
        ]
        n2 = 0
        fwd = {}
        for dx, dy in zip(XS, (1, -1, 2)):
            ax[dx].wait_recv()
            parts = []
            sx_, q0, q1 = xi(-dx), pl.ds(0, quart), pl.ds(quart, quart)
            for rows, d in ((lo, 1), (lo, -1), (q0, 2), (q1, -2)):
                r = fall.at[sx_, ylo, rows]
                parts.append(send(r, r, a2s.at[n2], a2r.at[n2], at_y(d)))
                n2 += 1
            fwd[("x", dx)] = parts
            for c in ay[dy]:
                c.wait_recv()
            parts = []
            for d in XS:
                r = fall.at[x, yi(-dy), hi]
                parts.append(send(r, r, a2s.at[n2], a2r.at[n2], at_x(d)))
                n2 += 1
            fwd[("y", dy)] = parts

    sc = jnp.where(core == 0, 1.0 / math.sqrt(width), 1.0 / math.sqrt(rank)).astype(F32)
    rate = jnp.where(core == 0, rate_down, rate_up).astype(F32)
    step_scale = 1.0 / math.sqrt(toks * roles * grps * tps)

    c_ls.wait()
    lane = lax.broadcasted_iota(jnp.int32, ls.shape, 1)
    ls_col = jnp.sum(jnp.where(lane == lindex[0], ls[...], 0.0), axis=1, keepdims=True)
    eye = lax.broadcasted_iota(jnp.int32, (rank, rank), 0) == lax.broadcasted_iota(jnp.int32, (rank, rank), 1)

    def to_row(col):
        return jnp.sum(jnp.where(eye, jnp.broadcast_to(col, (rank, rank)), 0.0), axis=0, keepdims=True)

    ls_row = to_row(ls_col)

    def operand(ix, iy):
        slot = ix * NY + iy
        return xbuf[:, :, pl.ds(pl.multiple_of(slot * cols, cols), cols)].reshape(2 * toks, cols)

    NT = (((1,), (1,)), ((), ()))

    with jax.named_scope("project"):
        c_x.wait()
        c_xs.wait_recv()

        def project(ix, iy):
            return lax.dot_general(fall[ix, iy], operand(ix, iy), NT, preferred_element_type=F32)

        acc = project(x, ylo)
        for dx in XS:
            acc = acc + project(xi(-dx), ylo)
        for dy in (1, -1, 2):
            acc = acc + project(x, yi(-dy))
        for dx, dy in [(dx, dy) for dx in XS for dy in (1, -1, 2)]:
            pieces = fwd[("x", dx)]
            for c in ([pieces[0]] if dy == 1 else [pieces[1]] if dy == -1 else pieces[2:]):
                c.wait_recv()
            fwd[("y", dy)][dx - 1].wait_recv()
            acc = acc + project(xi(-dx), yi(-dy))
        sx[core] = acc * sc

    with jax.named_scope("swap_projection"):
        c_s = send(sx.at[core], sx.at[core], ss.at[0], sr.at[0], sib)
        c_s.wait_recv()

    with jax.named_scope("gradient"):
        term = (sx[other] * ls_col).astype(BF16)
        c1 = {}
        n1 = 0

        def slice_gradient(ix, iy):
            return jnp.dot(term, operand(ix, iy), preferred_element_type=F32) * sc

        def send_x(dx, dy, n):
            return [send(gbuf.at[xi(dx), yi(dy), lo], rx.at[dx - 1, yi(dy)], c1s.at[n], c1r.at[n], at_x(dx))]

        def send_y(dx, dy, n):
            if dy != 2:
                i = 0 if dy == 1 else 1
                return [send(gbuf.at[xi(dx), yi(dy), hi], ry.at[i, xi(dx)], c1s.at[n], c1r.at[n], at_y(dy))]
            r0, r1 = pl.ds(half, quart), pl.ds(half + quart, quart)
            return [
                send(gbuf.at[xi(dx), yi(2), r0], ry.at[2, xi(dx), pl.ds(0, quart)], c1s.at[n], c1r.at[n], at_y(2)),
                send(gbuf.at[xi(dx), yi(2), r1], ry.at[2, xi(dx), pl.ds(quart, quart)], c1s.at[n + 1], c1r.at[n + 1], at_y(-2)),
            ]

        got_x, got_y = [], []
        order = [(dx, dy) for dx in (2, 1, 3) for dy in (2, 1, -1)] + [(dx, 0) for dx in (2, 1, 3)] + [(0, dy) for dy in (2, 1, -1)]
        for dx, dy in order:
            gbuf[xi(dx), yi(dy)] = slice_gradient(xi(dx), yi(dy)).astype(BF16)
            if dx:
                s_ = send_x(dx, dy, n1)
                n1 += len(s_)
                got_x += s_
            if dy:
                s_ = send_y(dx, dy, n1)
                n1 += len(s_)
                got_y += s_
        mine = slice_gradient(x, ylo)
        gbuf[x, ylo] = mine.astype(BF16)
        scale_row = to_row(jnp.sum(sx[0] * sx[1], axis=1, keepdims=True))

    with jax.named_scope("sum_plane_first"):
        for c in got_x:
            c.wait_recv()
        two = []

        def x_sum(iy):
            t = gbuf[x, iy, :half].astype(F32)
            for i in range(NX - 1):
                t = t + rx[i, iy].astype(F32)
            return t

        def y_sum(ix):
            t = gbuf[ix, ylo, half:].astype(F32)
            for i in range(NY - 1):
                t = t + ry[i, ix].astype(F32)
            return t

        for i, dy in enumerate((2, 1, -1)):
            p_src[i] = x_sum(yi(dy)).astype(BF16)
        two.append(send(p_src.at[0, pl.ds(0, quart)], ry2.at[0, pl.ds(0, quart)], c2s.at[0], c2r.at[0], at_y(2)))
        two.append(send(p_src.at[0, pl.ds(quart, quart)], ry2.at[0, pl.ds(quart, quart)], c2s.at[1], c2r.at[1], at_y(-2)))
        two.append(send(p_src.at[1], ry2.at[1], c2s.at[2], c2r.at[2], at_y(1)))
        two.append(send(p_src.at[2], ry2.at[2], c2s.at[3], c2r.at[3], at_y(-1)))
        top = x_sum(ylo)
        for c in got_y:
            c.wait_recv()
        for i, dx in enumerate((2, 1, 3)):
            p_src[3 + i] = y_sum(xi(dx)).astype(BF16)
            two.append(send(p_src.at[3 + i], rx2.at[i], c2s.at[4 + i], c2r.at[4 + i], at_x(dx)))
        bottom = y_sum(x)

    with jax.named_scope("send_cache"):
        head = tp // 2
        c_k.wait()
        c_v.wait()
        caches = []
        kv[:, tp] = kv_src[:, :, pl.ds(pl.multiple_of(head * HD, HD), HD)]
        for d in range(1, tps):
            to = (tp + d) % tps
            his = pl.ds(pl.multiple_of((to // 2) * HD, HD), HD)
            caches.append(
                send(kv_src.at[:, :, his], kv.at[:, tp], ks.at[d - 1], kr.at[d - 1], (role, grp, to))
            )

    with jax.named_scope("sum_plane_second"):
        for c in two:
            c.wait_recv()
        for i in range(3):
            top = top + ry2[i].astype(F32)
            bottom = bottom + rx2[i].astype(F32)
        s_hi = scale_row.astype(BF16).astype(F32)
        wide = jnp.concatenate([s_hi, scale_row - s_hi], axis=1)
        rb = rank // ZL
        rs_src[0:2, :, :cols] = top.reshape(ZL // 2, rb, cols).astype(BF16)
        rs_src[2:4, :, :cols] = bottom.reshape(ZL // 2, rb, cols).astype(BF16)
        rs_src[:, :, cols:] = jnp.broadcast_to(wide, (ZL, rb, 2 * rank)).astype(BF16)

    zb = z % ZL
    with jax.named_scope("sum_team"):
        team_c = []
        for i, (dz, dr) in reversed(list(enumerate(TEAM))):
            team_c.append(
                send(rs_src.at[(zb + dz + ZL) % ZL], rs_dst.at[i], r3s.at[i], r3r.at[i], at_z(dz, core, dr))
            )
        team_c.reverse()
        part = rs_src[zb].astype(F32)
        for i, c in enumerate(team_c):
            c.wait_recv()
            part = part + rs_dst[i].astype(F32)

    with jax.named_scope("sum_far"):

        def pack(v):
            s = v[:, cols:]
            s = s + pltpu.roll(s, rank, 1)
            h = s.astype(BF16).astype(F32)
            first = lax.broadcasted_iota(jnp.int32, s.shape, 1) < rank
            return jnp.where(first, h, s - h)

        z_src[:, :cols] = part[:, :cols].astype(BF16)
        z_src[:, cols:] = pack(part).astype(BF16)
        far_c = []
        for i, dz in enumerate(FAR):
            far_c.append(send(z_src, z_dst.at[i], r4s.at[i], r4r.at[i], at_z(dz, core)))
        part = z_src[...].astype(F32)
        mine_old = fall[x, ylo, pl.ds(pl.multiple_of(zb * rb, rb), rb)].astype(F32)
        for i, c in enumerate(far_c):
            c.wait_recv()
            part = part + z_dst[i].astype(F32)

    with jax.named_scope("spread_factors"):
        new = mine_old - (rate * step_scale) * part[:, :cols]
        nb[core, zb] = new.astype(BF16)
        spread = []
        blk = nb.at[core, zb]
        spread.append(send(blk, blk, n5s.at[0], n5r.at[0], sib))
        for i, dz in enumerate(NEAR):
            spread.append(send(blk, blk, n5s.at[1 + i], n5r.at[1 + i], at_z(dz, core)))
            spread.append(send(blk, blk, n5s.at[4 + i], n5r.at[4 + i], at_z(dz, other)))
        c_din.wait()
        drow = jnp.broadcast_to(
            din[:, pl.ds(pl.multiple_of(tp * cols, cols), cols)].astype(F32), (16, cols)
        ).astype(BF16)
        for c in spread:
            c.wait_recv()
        new_down = nb[0].reshape(rank, cols)
        new_up = nb[1].reshape(rank, cols)
        outs = [
            pltpu.make_async_copy(nb.at[0], ndown, oc.at[0]),
            pltpu.make_async_copy(nb.at[1], nup, oc.at[1]),
        ]
        for c in outs:
            c.start()

    with jax.named_scope("decode_hidden"):
        hid = lax.dot_general(drow, new_down, NT, preferred_element_type=F32)[:1]
        scale_part = part[:1, cols:cols + 2 * rank]
        scale_part = scale_part + pltpu.roll(scale_part, rank, 1)
        dh[tp] = jnp.concatenate([hid, scale_part[:, :rank]], axis=1)
        hid_c = []
        for d in range(1, tps):
            hid_c.append(send(dh.at[tp], dh.at[tp], dhs.at[d - 1], dhr.at[d - 1], (role, grp, (tp + d) % tps)))
        for c in hid_c:
            c.wait_recv()
        both = jnp.sum(dh[...], axis=0)
        scale_total = pltpu.roll(both, rank, 1)[:, :rank]
        new_scales = ls_row - (rate_scale * step_scale) * scale_total
        nscale[...] = new_scales
        dscaled = (both[:, :rank] * (1.0 / math.sqrt(width)) * new_scales)
        dscaled = jnp.broadcast_to(dscaled, (16, rank)).astype(BF16)
        c_bq.wait()
        q = jnp.dot(dscaled, new_up, preferred_element_type=F32)[:1] * (1.0 / math.sqrt(rank))
        q = bq[:, pl.ds(pl.multiple_of(tp * cols, cols), cols)].astype(F32) + q
        mine_n = cols // HD
        q = jnp.concatenate([q[:, h * HD:(h + 1) * HD] for h in range(mine_n)] + [jnp.zeros((16 - mine_n, HD), F32)], axis=0).astype(BF16)

    with jax.named_scope("attend"):
        c_fk.wait()
        c_fv.wait()
        for c in caches:
            c.wait_recv()
        hs = pl.ds(pl.multiple_of(head * HD, HD), HD)
        n_pos = tps * kv.shape[2]
        keys = kv[0].reshape(n_pos, HD)
        values = kv[1].reshape(n_pos, HD)
        key_scale = 1.0 / math.sqrt(HD)
        s = lax.dot_general(q, keys, NT, preferred_element_type=F32) * key_scale
        fresh = jnp.sum(q.astype(F32) * fk[:, hs].astype(F32), axis=1, keepdims=True) * key_scale
        live = lax.broadcasted_iota(jnp.int32, s.shape, 1) < lengths[0]
        high = jnp.maximum(jnp.max(jnp.where(live, s, -1e30), axis=1, keepdims=True), fresh)
        w = jnp.where(live, jnp.exp(s - high), 0.0)
        fw = jnp.exp(fresh - high)
        den = jnp.sum(w, axis=1, keepdims=True) + fw
        num = jnp.dot(w.astype(BF16), values, preferred_element_type=F32)
        num = num + fw.astype(BF16).astype(F32) * fv[:, hs].astype(F32)
        res = num / den
        atb[tp] = res[:mine_n]

    with jax.named_scope("spread_attended"):
        at_c = []
        for d in range(1, tps):
            at_c.append(send(atb.at[tp], atb.at[tp], ats.at[d - 1], atr.at[d - 1], (role, grp, (tp + d) % tps)))
        for c in at_c:
            c.wait_recv()
        for i in range(tps):
            rows = atb[i].astype(BF16)
            for h in range(mine_n):
                at = (i * mine_n + h) * HD
                att[:, at:at + HD] = rows[h:h + 1, :]

    with jax.named_scope("drain"):
        c_xs.wait_send()
        for c in sends:
            c.wait_send()
        for c in outs:
            c.wait()


def place(*refs):
    n = len(refs) // 2
    copies = [pltpu.make_async_copy(refs[i], refs[n + i], refs[-1].at[i]) for i in range(n)]
    for c in copies:
        c.start()
    for c in copies:
        c.wait()


def body(*args):
    learn, grad, fdown = args[0], args[1], args[2]
    roles, grps, tps = (lax.axis_size(a) for a in ("role", "grp", "tp"))
    rank, cols = fdown.shape
    toks, width = learn.shape
    local_pos = args[8].shape[1]
    n_far = grps // 2 // ZL - 1
    n_team = roles * ZL - 1
    mine_n = cols // HD
    kvw = args[10].shape[1]
    half, quart, rb = rank // 2, rank // 4, rank // ZL
    args = list(args)
    args[4] = args[4].T
    hbm = pl.BlockSpec(memory_space=pltpu.HBM)
    smem = pl.BlockSpec(memory_space=pltpu.SMEM)
    vmem = pl.BlockSpec(memory_space=pltpu.VMEM)
    in_specs = [hbm] * 5 + [smem] + [hbm] * 6 + [smem]
    dma = pltpu.SemaphoreType.DMA
    outs = pl.pallas_call(
        lambda *refs: kernel(roles, grps, tps, *refs),
        out_shape=(
            jax.ShapeDtypeStruct((ZL, rb, cols), BF16),
            jax.ShapeDtypeStruct((ZL, rb, cols), BF16),
            jax.ShapeDtypeStruct((1, rank), F32),
            jax.ShapeDtypeStruct((1, HEADS * HD), BF16),
        ),
        in_specs=in_specs,
        out_specs=(hbm, hbm, vmem, vmem),
        scratch_shapes=[
            pltpu.VMEM((2, toks, width), BF16),
            pltpu.VMEM((NX, NY, rank, cols), BF16),
            pltpu.VMEM((2, rank, 2 * toks), F32),
            pltpu.VMEM((NX, NY, rank, cols), BF16),
            pltpu.VMEM((NX - 1, NY, half, cols), BF16),
            pltpu.VMEM((NY - 1, NX, half, cols), BF16),
            pltpu.VMEM((6, half, cols), BF16),
            pltpu.VMEM((3, half, cols), BF16),
            pltpu.VMEM((3, half, cols), BF16),
            pltpu.VMEM((ZL, rb, cols + 2 * rank), BF16),
            pltpu.VMEM((n_team, rb, cols + 2 * rank), BF16),
            pltpu.VMEM((rb, cols + 2 * rank), BF16),
            pltpu.VMEM((n_far, rb, cols + 2 * rank), BF16),
            pltpu.VMEM((2, ZL, rb, cols), BF16),
            pltpu.VMEM((tps, 1, 2 * rank), F32),
            pltpu.VMEM((2, local_pos, kvw), BF16),
            pltpu.VMEM((2, tps, local_pos, HD), BF16),
            pltpu.VMEM((tps, mine_n, HD), F32),
            pltpu.VMEM(args[4].shape, F32),
            pltpu.VMEM((1, width), BF16),
            pltpu.VMEM((1, width), BF16),
            pltpu.VMEM((1, kvw), BF16),
            pltpu.VMEM((1, kvw), BF16),
            dma((9,)),
            dma((1,)), dma((1,)),
            dma((7,)), dma((7,)),
            dma((21,)), dma((21,)),
            dma((1,)), dma((1,)),
            dma((28,)), dma((28,)),
            dma((7,)), dma((7,)),
            dma((tps - 1,)), dma((tps - 1,)),
            dma((n_team,)), dma((n_team,)),
            dma((n_far,)), dma((n_far,)),
            dma((7,)), dma((7,)),
            dma((tps - 1,)), dma((tps - 1,)),
            dma((tps - 1,)), dma((tps - 1,)),
            dma((2,)),
        ],
        compiler_params=pltpu.CompilerParams(
            collective_id=0, has_side_effects=True, vmem_limit_bytes=60 * 1024 * 1024
        ),
    )(*args)
    results = (outs[0].reshape(rank, cols), outs[1].reshape(rank, cols), outs[2], outs[3])
    n = len(results)
    results = pl.pallas_call(
        place,
        out_shape=tuple(jax.ShapeDtypeStruct(r.shape, r.dtype) for r in results),
        in_specs=[hbm] * n,
        out_specs=(vmem,) * n,
        scratch_shapes=[dma((n,))],
    )(*results)
    return (results[0], results[1], results[2].reshape(rank), results[3])


def solution(mesh):
    in_specs = (
        P(("role", "grp", "tp"), None),
        P(("role", "grp", "tp"), None),
        P(None, "tp"),
        P(None, "tp"),
        P(),
        P(),
        P(("role", "grp"), None),
        P(("role", "grp"), None),
        P(("role", "grp"), "tp", None),
        P(("role", "grp"), "tp", None),
        P(("role", "grp"), None),
        P(("role", "grp"), None),
        P(("role", "grp")),
    )
    out_specs = (P(None, "tp"), P(None, "tp"), P(), P(("role", "grp"), None))
    return jax.shard_map(body, mesh=mesh, in_specs=in_specs, out_specs=out_specs, check_vma=False)
```

```python
import math

import jax
import jax.numpy as jnp
from jax import lax
from jax.experimental import pallas as pl
from jax.experimental.pallas import tpu as pltpu
from jax.sharding import PartitionSpec as P

HEADS = 64
KVH = 8
HD = 128

rate_down = 8.0
rate_up = 8.0
rate_scale = 0.1

MESH = pl.DeviceIdType.MESH
NX = 4
NY = 4
ZL = 4
F32 = jnp.float32
BF16 = jnp.bfloat16


def kernel(
    roles, grps, tps,
    learn, grad, fdown, fup, lscales, lindex, dinput, bquery, kcache, vcache, fkey, fvalue, lengths,
    ndown, nup, nscale, att,
    xbuf, fall, sx, gbuf, rx, ry, p_src, ry2, rx2, rs_src, rs_dst, z_src, z_dst, nb, dh, kv_src, kv, atb, ls, din, bq, fk, fv,
    loc, xs, xr, a1s, a1r, a2s, a2r, ss, sr, c1s, c1r, c2s, c2r, ks, kr, r3s, r3r, r4s, r4r, n5s, n5r, dhs, dhr, ats, atr, oc,
):
    rank, cols = fdown.shape
    toks, width = learn.shape
    zn = grps // 2
    half = rank // 2
    quart = rank // 4
    role = lax.axis_index("role")
    grp = lax.axis_index("grp")
    tp = lax.axis_index("tp")
    x, ylo = tp // NY, tp % NY
    y = role * NY + ylo
    z, core = grp // 2, grp % 2
    ny = roles * NY
    other = 1 - core
    sib = (role, z * 2 + other, tp)

    XS = tuple(range(1, NX))

    def at_x(dx):
        return (role, grp, (x + dx + NX) % NX * NY + ylo)

    def at_y(dy):
        yy = (y + dy + ny) % ny
        return (yy // NY, grp, x * NY + yy % NY)

    def xi(dx):
        return (x + dx + NX) % NX

    def yi(dy):
        return (ylo + dy + NY) % NY

    def at_z(dz, c, dr=0):
        return ((role + dr) % roles, (z + dz + zn) % zn * 2 + c, tp)

    local = []

    def fetch(src, dst):
        c = pltpu.make_async_copy(src, dst, loc.at[len(local)])
        c.start()
        local.append(c)
        return c

    sends = []

    def copy(src, dst, s, r, dev):
        return pltpu.make_async_remote_copy(
            src_ref=src, dst_ref=dst, send_sem=s, recv_sem=r, device_id=dev, device_id_type=MESH
        )

    def send(src, dst, s, r, dev):
        c = copy(src, dst, s, r, dev)
        c.start()
        sends.append(c)
        return c

    @pl.when(core == 0)
    def _():
        pltpu.make_async_copy(fdown, fall.at[x, ylo], loc.at[0]).start()
        pltpu.make_async_copy(learn, xbuf.at[core], loc.at[1]).start()

    @pl.when(core == 1)
    def _():
        pltpu.make_async_copy(fup, fall.at[x, ylo], loc.at[0]).start()
        pltpu.make_async_copy(grad, xbuf.at[core], loc.at[1]).start()

    c_f = pltpu.make_async_copy(fdown, fall.at[x, ylo], loc.at[0])
    c_x = pltpu.make_async_copy(learn, xbuf.at[core], loc.at[1])
    local.extend([c_f, c_x])
    c_k = fetch(kcache.at[0], kv_src.at[0])
    c_v = fetch(vcache.at[0], kv_src.at[1])
    c_ls = fetch(lscales, ls)
    c_din = fetch(dinput, din)
    c_bq = fetch(bquery, bq)
    c_fk = fetch(fkey, fk)
    c_fv = fetch(fvalue, fv)

    FAR = tuple(range(ZL, zn, ZL))
    NEAR = (1, -1, 2)
    TEAM = [(dz, dr) for dr in range(roles) for dz in (0,) + NEAR if dz or dr]

    with jax.named_scope("greet"):
        barrier = pltpu.get_barrier_semaphore()

        def greet(dev):
            pl.semaphore_signal(barrier, inc=1, device_id=dev, device_id_type=MESH)

        for dz, dr in reversed(TEAM):
            greet(at_z(-dz, core, dr))
        for dz in FAR:
            greet(at_z(-dz, core))
        for d in range(1, tps):
            greet((role, grp, (tp + d) % tps))
        for dz in NEAR:
            greet(at_z(-dz, other))
        for dy in (1, -1, 2, -2):
            greet(at_y(dy))
        greet(sib)
        pl.semaphore_wait(barrier, 1 + 4 + tps - 1 + len(TEAM) + len(NEAR) + len(FAR))

    head = tp // 2
    caches = []

    def send_cache(i, ds=None):
        for d in ds or range(1, tps):
            to = (tp + d) % tps
            his = pl.ds(pl.multiple_of((to // 2) * HD, HD), HD)
            n = i * (tps - 1) + d - 1
            caches.append(send(kv_src.at[i, :, his], kv.at[i, tp], ks.at[n], kr.at[n], (role, grp, to)))

    with jax.named_scope("send_own"):
        @pl.when(core == 0)
        def _():
            copy(grad, xbuf.at[core], xs.at[0], xr.at[0], sib).start()

        @pl.when(core == 1)
        def _():
            copy(learn, xbuf.at[core], xs.at[0], xr.at[0], sib).start()

        c_xs = copy(learn, xbuf.at[core], xs.at[0], xr.at[0], sib)
        c_f.wait()
        lo, hi = pl.ds(0, half), pl.ds(half, half)
        own = fall.at[x, ylo]
        ax = {dx: send(own, own, a1s.at[dx - 1], a1r.at[dx - 1], at_x(dx)) for dx in XS}
        ay = {
            1: [send(own, own, a1s.at[3], a1r.at[3], at_y(1))],
            -1: [send(own, own, a1s.at[4], a1r.at[4], at_y(-1))],
        }
        ay[2] = [
            send(fall.at[x, ylo, lo], fall.at[x, ylo, lo], a1s.at[5], a1r.at[5], at_y(2)),
            send(fall.at[x, ylo, hi], fall.at[x, ylo, hi], a1s.at[6], a1r.at[6], at_y(-2)),
        ]
        n2 = 0
        fwd = {}
        for dx, dy in zip(XS, (1, -1, 2)):
            ax[dx].wait_recv()
            parts = []
            sx_, q0, q1 = xi(-dx), pl.ds(0, quart), pl.ds(quart, quart)
            for rows, d in ((lo, 1), (lo, -1), (q0, 2), (q1, -2)):
                r = fall.at[sx_, ylo, rows]
                parts.append(send(r, r, a2s.at[n2], a2r.at[n2], at_y(d)))
                n2 += 1
            fwd[("x", dx)] = parts
            for c in ay[dy]:
                c.wait_recv()
            parts = []
            for d in XS:
                r = fall.at[x, yi(-dy), hi]
                parts.append(send(r, r, a2s.at[n2], a2r.at[n2], at_x(d)))
                n2 += 1
            fwd[("y", dy)] = parts

    with jax.named_scope("send_cache"):
        c_k.wait()
        c_v.wait()
        kv[:, tp] = kv_src[:, :, pl.ds(pl.multiple_of(head * HD, HD), HD)]

    sc = jnp.where(core == 0, 1.0 / math.sqrt(width), 1.0 / math.sqrt(rank)).astype(F32)
    rate = jnp.where(core == 0, rate_down, rate_up).astype(F32)
    step_scale = 1.0 / math.sqrt(toks * roles * grps * tps)

    c_ls.wait()
    lane = lax.broadcasted_iota(jnp.int32, ls.shape, 1)
    ls_col = jnp.sum(jnp.where(lane == lindex[0], ls[...], 0.0), axis=1, keepdims=True)
    eye = lax.broadcasted_iota(jnp.int32, (rank, rank), 0) == lax.broadcasted_iota(jnp.int32, (rank, rank), 1)

    def to_row(col):
        return jnp.sum(jnp.where(eye, jnp.broadcast_to(col, (rank, rank)), 0.0), axis=0, keepdims=True)

    ls_row = to_row(ls_col)

    def operand(ix, iy):
        slot = ix * NY + iy
        return xbuf[:, :, pl.ds(pl.multiple_of(slot * cols, cols), cols)].reshape(2 * toks, cols)

    NT = (((1,), (1,)), ((), ()))

    with jax.named_scope("project"):
        c_x.wait()
        c_xs.wait_recv()

        def project(ix, iy):
            return lax.dot_general(fall[ix, iy], operand(ix, iy), NT, preferred_element_type=F32)

        acc = project(x, ylo)
        for dx in XS:
            acc = acc + project(xi(-dx), ylo)
        for dy in (1, -1, 2):
            acc = acc + project(x, yi(-dy))
        for dx, dy in [(dx, dy) for dx in XS for dy in (1, -1, 2)]:
            pieces = fwd[("x", dx)]
            for c in ([pieces[0]] if dy == 1 else [pieces[1]] if dy == -1 else pieces[2:]):
                c.wait_recv()
            fwd[("y", dy)][dx - 1].wait_recv()
            acc = acc + project(xi(-dx), yi(-dy))
        sx[core] = acc * sc

    with jax.named_scope("swap_projection"):
        c_s = send(sx.at[core], sx.at[core], ss.at[0], sr.at[0], sib)
        c_s.wait_recv()

    with jax.named_scope("gradient"):
        term = (sx[other] * ls_col).astype(BF16)
        c1 = {}
        n1 = 0

        def slice_gradient(ix, iy):
            return jnp.dot(term, operand(ix, iy), preferred_element_type=F32) * sc

        def send_x(dx, dy, n):
            return [send(gbuf.at[xi(dx), yi(dy), lo], rx.at[dx - 1, yi(dy)], c1s.at[n], c1r.at[n], at_x(dx))]

        def send_y(dx, dy, n):
            if dy != 2:
                i = 0 if dy == 1 else 1
                return [send(gbuf.at[xi(dx), yi(dy), hi], ry.at[i, xi(dx)], c1s.at[n], c1r.at[n], at_y(dy))]
            r0, r1 = pl.ds(half, quart), pl.ds(half + quart, quart)
            return [
                send(gbuf.at[xi(dx), yi(2), r0], ry.at[2, xi(dx), pl.ds(0, quart)], c1s.at[n], c1r.at[n], at_y(2)),
                send(gbuf.at[xi(dx), yi(2), r1], ry.at[2, xi(dx), pl.ds(quart, quart)], c1s.at[n + 1], c1r.at[n + 1], at_y(-2)),
            ]

        got_x, got_y = [], []
        order = [(dx, dy) for dx in (2, 1, 3) for dy in (2, 1, -1)] + [(dx, 0) for dx in (2, 1, 3)] + [(0, dy) for dy in (2, 1, -1)]
        for dx, dy in order:
            gbuf[xi(dx), yi(dy)] = slice_gradient(xi(dx), yi(dy)).astype(BF16)
            if dx:
                s_ = send_x(dx, dy, n1)
                n1 += len(s_)
                got_x += s_
            if dy:
                s_ = send_y(dx, dy, n1)
                n1 += len(s_)
                got_y += s_
        mine = slice_gradient(x, ylo)
        gbuf[x, ylo] = mine.astype(BF16)
        scale_row = to_row(jnp.sum(sx[0] * sx[1], axis=1, keepdims=True))

    with jax.named_scope("sum_plane_first"):
        for c in got_x:
            c.wait_recv()
        two = []

        def x_sum(iy):
            t = gbuf[x, iy, :half].astype(F32)
            for i in range(NX - 1):
                t = t + rx[i, iy].astype(F32)
            return t

        def y_sum(ix):
            t = gbuf[ix, ylo, half:].astype(F32)
            for i in range(NY - 1):
                t = t + ry[i, ix].astype(F32)
            return t

        for i, dy in enumerate((2, 1, -1)):
            p_src[i] = x_sum(yi(dy)).astype(BF16)
        two.append(send(p_src.at[0, pl.ds(0, quart)], ry2.at[0, pl.ds(0, quart)], c2s.at[0], c2r.at[0], at_y(2)))
        two.append(send(p_src.at[0, pl.ds(quart, quart)], ry2.at[0, pl.ds(quart, quart)], c2s.at[1], c2r.at[1], at_y(-2)))
        two.append(send(p_src.at[1], ry2.at[1], c2s.at[2], c2r.at[2], at_y(1)))
        two.append(send(p_src.at[2], ry2.at[2], c2s.at[3], c2r.at[3], at_y(-1)))
        top = x_sum(ylo)
        for c in got_y:
            c.wait_recv()
        for i, dx in enumerate((2, 1, 3)):
            p_src[3 + i] = y_sum(xi(dx)).astype(BF16)
            two.append(send(p_src.at[3 + i], rx2.at[i], c2s.at[4 + i], c2r.at[4 + i], at_x(dx)))
        bottom = y_sum(x)

    with jax.named_scope("sum_plane_second"):
        for c in two:
            c.wait_recv()
        for i in range(3):
            top = top + ry2[i].astype(F32)
            bottom = bottom + rx2[i].astype(F32)
        s_hi = scale_row.astype(BF16).astype(F32)
        wide = jnp.concatenate([s_hi, scale_row - s_hi], axis=1)
        rb = rank // ZL
        rs_src[0:2, :, :cols] = top.reshape(ZL // 2, rb, cols).astype(BF16)
        rs_src[2:4, :, :cols] = bottom.reshape(ZL // 2, rb, cols).astype(BF16)
        rs_src[:, :, cols:] = jnp.broadcast_to(wide, (ZL, rb, 2 * rank)).astype(BF16)

    zb = z % ZL
    with jax.named_scope("sum_team"):
        team_c = []
        for i, (dz, dr) in reversed(list(enumerate(TEAM))):
            team_c.append(
                send(rs_src.at[(zb + dz + ZL) % ZL], rs_dst.at[i], r3s.at[i], r3r.at[i], at_z(dz, core, dr))
            )
        team_c.reverse()
        part = rs_src[zb].astype(F32)
        for i, c in enumerate(team_c):
            c.wait_recv()
            part = part + rs_dst[i].astype(F32)

    with jax.named_scope("sum_far"):

        def pack(v):
            s = v[:, cols:]
            s = s + pltpu.roll(s, rank, 1)
            h = s.astype(BF16).astype(F32)
            first = lax.broadcasted_iota(jnp.int32, s.shape, 1) < rank
            return jnp.where(first, h, s - h)

        z_src[:, :cols] = part[:, :cols].astype(BF16)
        z_src[:, cols:] = pack(part).astype(BF16)
        far_c = []
        for i, dz in enumerate(FAR):
            far_c.append(send(z_src, z_dst.at[i], r4s.at[i], r4r.at[i], at_z(dz, core)))
        send_cache(0)
        send_cache(1)
        part = z_src[...].astype(F32)
        mine_old = fall[x, ylo, pl.ds(pl.multiple_of(zb * rb, rb), rb)].astype(F32)
        for i, c in enumerate(far_c):
            c.wait_recv()
            part = part + z_dst[i].astype(F32)

    with jax.named_scope("spread_factors"):
        new = mine_old - (rate * step_scale) * part[:, :cols]
        nb[core, zb] = new.astype(BF16)
        spread = []
        blk = nb.at[core, zb]
        spread.append(send(blk, blk, n5s.at[0], n5r.at[0], sib))
        for i, dz in enumerate(NEAR):
            spread.append(send(blk, blk, n5s.at[1 + i], n5r.at[1 + i], at_z(dz, core)))
            spread.append(send(blk, blk, n5s.at[4 + i], n5r.at[4 + i], at_z(dz, other)))
        c_din.wait()
        drow = jnp.broadcast_to(
            din[:, pl.ds(pl.multiple_of(tp * cols, cols), cols)].astype(F32), (16, cols)
        ).astype(BF16)
        for c in spread:
            c.wait_recv()
        new_down = nb[0].reshape(rank, cols)
        new_up = nb[1].reshape(rank, cols)
        outs = [
            pltpu.make_async_copy(nb.at[0], ndown, oc.at[0]),
            pltpu.make_async_copy(nb.at[1], nup, oc.at[1]),
        ]
        for c in outs:
            c.start()

    with jax.named_scope("decode_hidden"):
        hid = lax.dot_general(drow, new_down, NT, preferred_element_type=F32)[:1]
        scale_part = part[:1, cols:cols + 2 * rank]
        scale_part = scale_part + pltpu.roll(scale_part, rank, 1)
        dh[tp] = jnp.concatenate([hid, scale_part[:, :rank]], axis=1)
        hid_c = []
        for d in range(1, tps):
            hid_c.append(send(dh.at[tp], dh.at[tp], dhs.at[d - 1], dhr.at[d - 1], (role, grp, (tp + d) % tps)))
        for c in hid_c:
            c.wait_recv()
        both = jnp.sum(dh[...], axis=0)
        scale_total = pltpu.roll(both, rank, 1)[:, :rank]
        new_scales = ls_row - (rate_scale * step_scale) * scale_total
        nscale[...] = new_scales
        dscaled = (both[:, :rank] * (1.0 / math.sqrt(width)) * new_scales)
        dscaled = jnp.broadcast_to(dscaled, (16, rank)).astype(BF16)
        c_bq.wait()
        q = jnp.dot(dscaled, new_up, preferred_element_type=F32)[:1] * (1.0 / math.sqrt(rank))
        q = bq[:, pl.ds(pl.multiple_of(tp * cols, cols), cols)].astype(F32) + q
        mine_n = cols // HD
        q = jnp.concatenate([q[:, h * HD:(h + 1) * HD] for h in range(mine_n)] + [jnp.zeros((16 - mine_n, HD), F32)], axis=0).astype(BF16)

    with jax.named_scope("attend"):
        c_fk.wait()
        c_fv.wait()
        for c in caches:
            c.wait_recv()
        hs = pl.ds(pl.multiple_of(head * HD, HD), HD)
        n_pos = tps * kv.shape[2]
        keys = kv[0].reshape(n_pos, HD)
        values = kv[1].reshape(n_pos, HD)
        key_scale = 1.0 / math.sqrt(HD)
        s = lax.dot_general(q, keys, NT, preferred_element_type=F32) * key_scale
        fresh = jnp.sum(q.astype(F32) * fk[:, hs].astype(F32), axis=1, keepdims=True) * key_scale
        live = lax.broadcasted_iota(jnp.int32, s.shape, 1) < lengths[0]
        high = jnp.maximum(jnp.max(jnp.where(live, s, -1e30), axis=1, keepdims=True), fresh)
        w = jnp.where(live, jnp.exp(s - high), 0.0)
        fw = jnp.exp(fresh - high)
        den = jnp.sum(w, axis=1, keepdims=True) + fw
        num = jnp.dot(w.astype(BF16), values, preferred_element_type=F32)
        num = num + fw.astype(BF16).astype(F32) * fv[:, hs].astype(F32)
        res = num / den
        atb[tp] = res[:mine_n]

    with jax.named_scope("spread_attended"):
        at_c = []
        for d in range(1, tps):
            at_c.append(send(atb.at[tp], atb.at[tp], ats.at[d - 1], atr.at[d - 1], (role, grp, (tp + d) % tps)))
        for c in at_c:
            c.wait_recv()
        for i in range(tps):
            rows = atb[i].astype(BF16)
            for h in range(mine_n):
                at = (i * mine_n + h) * HD
                att[:, at:at + HD] = rows[h:h + 1, :]

    with jax.named_scope("drain"):
        c_xs.wait_send()
        for c in sends:
            c.wait_send()
        for c in outs:
            c.wait()


def place(*refs):
    n = len(refs) // 2
    copies = [pltpu.make_async_copy(refs[i], refs[n + i], refs[-1].at[i]) for i in range(n)]
    for c in copies:
        c.start()
    for c in copies:
        c.wait()


def body(*args):
    learn, grad, fdown = args[0], args[1], args[2]
    roles, grps, tps = (lax.axis_size(a) for a in ("role", "grp", "tp"))
    rank, cols = fdown.shape
    toks, width = learn.shape
    local_pos = args[8].shape[1]
    n_far = grps // 2 // ZL - 1
    n_team = roles * ZL - 1
    mine_n = cols // HD
    kvw = args[10].shape[1]
    half, quart, rb = rank // 2, rank // 4, rank // ZL
    args = list(args)
    args[4] = args[4].T
    hbm = pl.BlockSpec(memory_space=pltpu.HBM)
    smem = pl.BlockSpec(memory_space=pltpu.SMEM)
    vmem = pl.BlockSpec(memory_space=pltpu.VMEM)
    in_specs = [hbm] * 5 + [smem] + [hbm] * 6 + [smem]
    dma = pltpu.SemaphoreType.DMA
    outs = pl.pallas_call(
        lambda *refs: kernel(roles, grps, tps, *refs),
        out_shape=(
            jax.ShapeDtypeStruct((ZL, rb, cols), BF16),
            jax.ShapeDtypeStruct((ZL, rb, cols), BF16),
            jax.ShapeDtypeStruct((1, rank), F32),
            jax.ShapeDtypeStruct((1, HEADS * HD), BF16),
        ),
        in_specs=in_specs,
        out_specs=(hbm, hbm, vmem, vmem),
        scratch_shapes=[
            pltpu.VMEM((2, toks, width), BF16),
            pltpu.VMEM((NX, NY, rank, cols), BF16),
            pltpu.VMEM((2, rank, 2 * toks), F32),
            pltpu.VMEM((NX, NY, rank, cols), BF16),
            pltpu.VMEM((NX - 1, NY, half, cols), BF16),
            pltpu.VMEM((NY - 1, NX, half, cols), BF16),
            pltpu.VMEM((6, half, cols), BF16),
            pltpu.VMEM((3, half, cols), BF16),
            pltpu.VMEM((3, half, cols), BF16),
            pltpu.VMEM((ZL, rb, cols + 2 * rank), BF16),
            pltpu.VMEM((n_team, rb, cols + 2 * rank), BF16),
            pltpu.VMEM((rb, cols + 2 * rank), BF16),
            pltpu.VMEM((n_far, rb, cols + 2 * rank), BF16),
            pltpu.VMEM((2, ZL, rb, cols), BF16),
            pltpu.VMEM((tps, 1, 2 * rank), F32),
            pltpu.VMEM((2, local_pos, kvw), BF16),
            pltpu.VMEM((2, tps, local_pos, HD), BF16),
            pltpu.VMEM((tps, mine_n, HD), F32),
            pltpu.VMEM(args[4].shape, F32),
            pltpu.VMEM((1, width), BF16),
            pltpu.VMEM((1, width), BF16),
            pltpu.VMEM((1, kvw), BF16),
            pltpu.VMEM((1, kvw), BF16),
            dma((9,)),
            dma((1,)), dma((1,)),
            dma((7,)), dma((7,)),
            dma((21,)), dma((21,)),
            dma((1,)), dma((1,)),
            dma((28,)), dma((28,)),
            dma((7,)), dma((7,)),
            dma((2 * tps - 2,)), dma((2 * tps - 2,)),
            dma((n_team,)), dma((n_team,)),
            dma((n_far,)), dma((n_far,)),
            dma((7,)), dma((7,)),
            dma((tps - 1,)), dma((tps - 1,)),
            dma((tps - 1,)), dma((tps - 1,)),
            dma((2,)),
        ],
        compiler_params=pltpu.CompilerParams(
            collective_id=0, has_side_effects=True, vmem_limit_bytes=60 * 1024 * 1024
        ),
    )(*args)
    results = (outs[0].reshape(rank, cols), outs[1].reshape(rank, cols), outs[2], outs[3])
    n = len(results)
    results = pl.pallas_call(
        place,
        out_shape=tuple(jax.ShapeDtypeStruct(r.shape, r.dtype) for r in results),
        in_specs=[hbm] * n,
        out_specs=(vmem,) * n,
        scratch_shapes=[dma((n,))],
    )(*results)
    return (results[0], results[1], results[2].reshape(rank), results[3])


def solution(mesh):
    in_specs = (
        P(("role", "grp", "tp"), None),
        P(("role", "grp", "tp"), None),
        P(None, "tp"),
        P(None, "tp"),
        P(),
        P(),
        P(("role", "grp"), None),
        P(("role", "grp"), None),
        P(("role", "grp"), "tp", None),
        P(("role", "grp"), "tp", None),
        P(("role", "grp"), None),
        P(("role", "grp"), None),
        P(("role", "grp")),
    )
    out_specs = (P(None, "tp"), P(None, "tp"), P(), P(("role", "grp"), None))
    return jax.shard_map(body, mesh=mesh, in_specs=in_specs, out_specs=out_specs, check_vma=False)
```

```python
import math

import jax
import jax.numpy as jnp
from jax import lax
from jax.experimental import pallas as pl
from jax.experimental.pallas import tpu as pltpu
from jax.sharding import PartitionSpec as P

HEADS = 64
KVH = 8
HD = 128

rate_down = 8.0
rate_up = 8.0
rate_scale = 0.1

MESH = pl.DeviceIdType.MESH
NX = 4
NY = 4
ZL = 4
F32 = jnp.float32
BF16 = jnp.bfloat16


def kernel(
    roles, grps, tps,
    learn, grad, fdown, fup, lscales, lindex, dinput, bquery, kcache, vcache, fkey, fvalue, lengths,
    ndown, nup, nscale, att,
    xbuf, fall, sx, gbuf, rx, ry, p_src, ry2, rx2, rs_src, rs_dst, z_src, z_dst, nb, dh, kv_src, kv, atb, ls, din, bq, fk, fv,
    loc, xs, xr, a1s, a1r, a2s, a2r, ss, sr, c1s, c1r, c2s, c2r, ks, kr, r3s, r3r, r4s, r4r, n5s, n5r, dhs, dhr, ats, atr, oc,
):
    rank, cols = fdown.shape
    toks, width = learn.shape
    zn = grps // 2
    half = rank // 2
    quart = rank // 4
    role = lax.axis_index("role")
    grp = lax.axis_index("grp")
    tp = lax.axis_index("tp")
    x, ylo = tp // NY, tp % NY
    y = role * NY + ylo
    z, core = grp // 2, grp % 2
    ny = roles * NY
    other = 1 - core
    sib = (role, z * 2 + other, tp)

    XS = tuple(range(1, NX))

    def at_x(dx):
        return (role, grp, (x + dx + NX) % NX * NY + ylo)

    def at_y(dy):
        yy = (y + dy + ny) % ny
        return (yy // NY, grp, x * NY + yy % NY)

    def xi(dx):
        return (x + dx + NX) % NX

    def yi(dy):
        return (ylo + dy + NY) % NY

    def at_z(dz, c, dr=0):
        return ((role + dr) % roles, (z + dz + zn) % zn * 2 + c, tp)

    local = []

    def fetch(src, dst):
        c = pltpu.make_async_copy(src, dst, loc.at[len(local)])
        c.start()
        local.append(c)
        return c

    sends = []

    def copy(src, dst, s, r, dev):
        return pltpu.make_async_remote_copy(
            src_ref=src, dst_ref=dst, send_sem=s, recv_sem=r, device_id=dev, device_id_type=MESH
        )

    def send(src, dst, s, r, dev):
        c = copy(src, dst, s, r, dev)
        c.start()
        sends.append(c)
        return c

    @pl.when(core == 0)
    def _():
        pltpu.make_async_copy(fdown, fall.at[x, ylo], loc.at[0]).start()
        pltpu.make_async_copy(learn, xbuf.at[core], loc.at[1]).start()

    @pl.when(core == 1)
    def _():
        pltpu.make_async_copy(fup, fall.at[x, ylo], loc.at[0]).start()
        pltpu.make_async_copy(grad, xbuf.at[core], loc.at[1]).start()

    c_f = pltpu.make_async_copy(fdown, fall.at[x, ylo], loc.at[0])
    c_x = pltpu.make_async_copy(learn, xbuf.at[core], loc.at[1])
    local.extend([c_f, c_x])
    c_k = fetch(kcache.at[0], kv_src.at[0])
    c_v = fetch(vcache.at[0], kv_src.at[1])
    c_ls = fetch(lscales, ls)
    c_din = fetch(dinput, din)
    c_bq = fetch(bquery, bq)
    c_fk = fetch(fkey, fk)
    c_fv = fetch(fvalue, fv)

    FAR = tuple(range(ZL, zn, ZL))
    NEAR = (1, -1, 2)
    TEAM = [(dz, dr) for dr in range(roles) for dz in (0,) + NEAR if dz or dr]

    with jax.named_scope("greet"):
        barrier = pltpu.get_barrier_semaphore()

        def greet(dev):
            pl.semaphore_signal(barrier, inc=1, device_id=dev, device_id_type=MESH)

        for dz, dr in reversed(TEAM):
            greet(at_z(-dz, core, dr))
        for dz in FAR:
            greet(at_z(-dz, core))
        for d in range(1, tps):
            greet((role, grp, (tp + d) % tps))
        for dz in NEAR:
            greet(at_z(-dz, other))
        for dy in (1, -1, 2, -2):
            greet(at_y(dy))
        greet(sib)
        pl.semaphore_wait(barrier, 1 + 4 + tps - 1 + len(TEAM) + len(NEAR) + len(FAR))

    head = tp // 2
    caches = []

    def send_cache(i, ds=None):
        for d in ds or range(1, tps):
            to = (tp + d) % tps
            his = pl.ds(pl.multiple_of((to // 2) * HD, HD), HD)
            n = i * (tps - 1) + d - 1
            caches.append(send(kv_src.at[i, :, his], kv.at[i, tp], ks.at[n], kr.at[n], (role, grp, to)))

    with jax.named_scope("send_own"):
        @pl.when(core == 0)
        def _():
            copy(grad, xbuf.at[core], xs.at[0], xr.at[0], sib).start()

        @pl.when(core == 1)
        def _():
            copy(learn, xbuf.at[core], xs.at[0], xr.at[0], sib).start()

        c_xs = copy(learn, xbuf.at[core], xs.at[0], xr.at[0], sib)
        c_f.wait()
        lo, hi = pl.ds(0, half), pl.ds(half, half)
        own = fall.at[x, ylo]
        ax = {dx: send(own, own, a1s.at[dx - 1], a1r.at[dx - 1], at_x(dx)) for dx in XS}
        ay = {
            1: [send(own, own, a1s.at[3], a1r.at[3], at_y(1))],
            -1: [send(own, own, a1s.at[4], a1r.at[4], at_y(-1))],
        }
        ay[2] = [
            send(fall.at[x, ylo, lo], fall.at[x, ylo, lo], a1s.at[5], a1r.at[5], at_y(2)),
            send(fall.at[x, ylo, hi], fall.at[x, ylo, hi], a1s.at[6], a1r.at[6], at_y(-2)),
        ]
        n2 = 0
        fwd = {}
        for dx, dy in zip(XS, (1, -1, 2)):
            ax[dx].wait_recv()
            parts = []
            sx_, q0, q1 = xi(-dx), pl.ds(0, quart), pl.ds(quart, quart)
            for rows, d in ((lo, 1), (lo, -1), (q0, 2), (q1, -2)):
                r = fall.at[sx_, ylo, rows]
                parts.append(send(r, r, a2s.at[n2], a2r.at[n2], at_y(d)))
                n2 += 1
            fwd[("x", dx)] = parts
            for c in ay[dy]:
                c.wait_recv()
            parts = []
            for d in XS:
                r = fall.at[x, yi(-dy), hi]
                parts.append(send(r, r, a2s.at[n2], a2r.at[n2], at_x(d)))
                n2 += 1
            fwd[("y", dy)] = parts

    with jax.named_scope("send_cache"):
        c_k.wait()
        c_v.wait()
        kv[:, tp] = kv_src[:, :, pl.ds(pl.multiple_of(head * HD, HD), HD)]

    sc = jnp.where(core == 0, 1.0 / math.sqrt(width), 1.0 / math.sqrt(rank)).astype(F32)
    rate = jnp.where(core == 0, rate_down, rate_up).astype(F32)
    step_scale = 1.0 / math.sqrt(toks * roles * grps * tps)

    c_ls.wait()
    lane = lax.broadcasted_iota(jnp.int32, ls.shape, 1)
    ls_col = jnp.sum(jnp.where(lane == lindex[0], ls[...], 0.0), axis=1, keepdims=True)
    eye = lax.broadcasted_iota(jnp.int32, (rank, rank), 0) == lax.broadcasted_iota(jnp.int32, (rank, rank), 1)

    def to_row(col):
        return jnp.sum(jnp.where(eye, jnp.broadcast_to(col, (rank, rank)), 0.0), axis=0, keepdims=True)

    ls_row = to_row(ls_col)

    def operand(ix, iy):
        slot = ix * NY + iy
        return xbuf[:, :, pl.ds(pl.multiple_of(slot * cols, cols), cols)].reshape(2 * toks, cols)

    NT = (((1,), (1,)), ((), ()))

    with jax.named_scope("project"):
        c_x.wait()
        c_xs.wait_recv()

        def project(ix, iy):
            return lax.dot_general(fall[ix, iy], operand(ix, iy), NT, preferred_element_type=F32)

        acc = project(x, ylo)
        for dx in XS:
            acc = acc + project(xi(-dx), ylo)
        for dy in (1, -1, 2):
            acc = acc + project(x, yi(-dy))
        for dx, dy in [(dx, dy) for dx in XS for dy in (1, -1, 2)]:
            pieces = fwd[("x", dx)]
            for c in ([pieces[0]] if dy == 1 else [pieces[1]] if dy == -1 else pieces[2:]):
                c.wait_recv()
            fwd[("y", dy)][dx - 1].wait_recv()
            acc = acc + project(xi(-dx), yi(-dy))
        sx[core] = acc * sc

    with jax.named_scope("swap_projection"):
        c_s = send(sx.at[core], sx.at[core], ss.at[0], sr.at[0], sib)
        c_s.wait_recv()

    with jax.named_scope("gradient"):
        term = (sx[other] * ls_col).astype(BF16)
        c1 = {}
        n1 = 0

        def slice_gradient(ix, iy):
            return jnp.dot(term, operand(ix, iy), preferred_element_type=F32) * sc

        def send_x(dx, dy, n):
            return [send(gbuf.at[xi(dx), yi(dy), lo], rx.at[dx - 1, yi(dy)], c1s.at[n], c1r.at[n], at_x(dx))]

        def send_y(dx, dy, n):
            if dy != 2:
                i = 0 if dy == 1 else 1
                return [send(gbuf.at[xi(dx), yi(dy), hi], ry.at[i, xi(dx)], c1s.at[n], c1r.at[n], at_y(dy))]
            r0, r1 = pl.ds(half, quart), pl.ds(half + quart, quart)
            return [
                send(gbuf.at[xi(dx), yi(2), r0], ry.at[2, xi(dx), pl.ds(0, quart)], c1s.at[n], c1r.at[n], at_y(2)),
                send(gbuf.at[xi(dx), yi(2), r1], ry.at[2, xi(dx), pl.ds(quart, quart)], c1s.at[n + 1], c1r.at[n + 1], at_y(-2)),
            ]

        got_x, got_y = {}, {}
        order = [(2, 2), (1, 2), (2, 1), (3, 2), (2, -1), (0, 2), (2, 0)]
        order += [(1, 1), (3, 1), (1, -1), (3, -1), (0, 1), (1, 0), (0, -1), (3, 0)]
        for dx, dy in order:
            gbuf[xi(dx), yi(dy)] = slice_gradient(xi(dx), yi(dy)).astype(BF16)
            if dx:
                s_ = send_x(dx, dy, n1)
                n1 += len(s_)
                got_x[dx, dy] = s_
            if dy:
                s_ = send_y(dx, dy, n1)
                n1 += len(s_)
                got_y[dx, dy] = s_
        mine = slice_gradient(x, ylo)
        gbuf[x, ylo] = mine.astype(BF16)
        scale_row = to_row(jnp.sum(sx[0] * sx[1], axis=1, keepdims=True))

    with jax.named_scope("sum_plane_first"):
        two = []

        def x_sum(dy):
            for i in XS:
                for c in got_x[i, dy]:
                    c.wait_recv()
            iy = yi(dy)
            t = gbuf[x, iy, :half].astype(F32)
            for i in range(NX - 1):
                t = t + rx[i, iy].astype(F32)
            return t

        def y_sum(dx):
            for i in (2, 1, -1):
                for c in got_y[dx, i]:
                    c.wait_recv()
            ix = xi(dx)
            t = gbuf[ix, ylo, half:].astype(F32)
            for i in range(NY - 1):
                t = t + ry[i, ix].astype(F32)
            return t

        for i, (dx, dy) in enumerate(((2, 2), (1, 1), (3, -1))):
            p_src[i] = x_sum(dy).astype(BF16)
            if dy == 2:
                for k, d in enumerate((2, -2)):
                    r = pl.ds(k * quart, quart)
                    two.append(send(p_src.at[0, r], ry2.at[0, r], c2s.at[k], c2r.at[k], at_y(d)))
            else:
                two.append(send(p_src.at[i], ry2.at[i], c2s.at[1 + i], c2r.at[1 + i], at_y(dy)))
            p_src[3 + i] = y_sum(dx).astype(BF16)
            two.append(send(p_src.at[3 + i], rx2.at[i], c2s.at[4 + i], c2r.at[4 + i], at_x(dx)))
        top = x_sum(0)
        bottom = y_sum(0)

    with jax.named_scope("sum_plane_second"):
        for c in two:
            c.wait_recv()
        for i in range(3):
            top = top + ry2[i].astype(F32)
            bottom = bottom + rx2[i].astype(F32)
        s_hi = scale_row.astype(BF16).astype(F32)
        wide = jnp.concatenate([s_hi, scale_row - s_hi], axis=1)
        rb = rank // ZL
        rs_src[0:2, :, :cols] = top.reshape(ZL // 2, rb, cols).astype(BF16)
        rs_src[2:4, :, :cols] = bottom.reshape(ZL // 2, rb, cols).astype(BF16)
        rs_src[:, :, cols:] = jnp.broadcast_to(wide, (ZL, rb, 2 * rank)).astype(BF16)

    zb = z % ZL
    with jax.named_scope("sum_team"):
        team_c = []
        for i, (dz, dr) in reversed(list(enumerate(TEAM))):
            team_c.append(
                send(rs_src.at[(zb + dz + ZL) % ZL], rs_dst.at[i], r3s.at[i], r3r.at[i], at_z(dz, core, dr))
            )
        team_c.reverse()
        part = rs_src[zb].astype(F32)
        for i, c in enumerate(team_c):
            c.wait_recv()
            part = part + rs_dst[i].astype(F32)

    with jax.named_scope("sum_far"):

        def pack(v):
            s = v[:, cols:]
            s = s + pltpu.roll(s, rank, 1)
            h = s.astype(BF16).astype(F32)
            first = lax.broadcasted_iota(jnp.int32, s.shape, 1) < rank
            return jnp.where(first, h, s - h)

        z_src[:, :cols] = part[:, :cols].astype(BF16)
        z_src[:, cols:] = pack(part).astype(BF16)
        far_c = []
        for i, dz in enumerate(FAR):
            far_c.append(send(z_src, z_dst.at[i], r4s.at[i], r4r.at[i], at_z(dz, core)))
        send_cache(0)
        send_cache(1)
        part = z_src[...].astype(F32)
        mine_old = fall[x, ylo, pl.ds(pl.multiple_of(zb * rb, rb), rb)].astype(F32)
        for i, c in enumerate(far_c):
            c.wait_recv()
            part = part + z_dst[i].astype(F32)

    with jax.named_scope("spread_factors"):
        new = mine_old - (rate * step_scale) * part[:, :cols]
        nb[core, zb] = new.astype(BF16)
        spread = []
        blk = nb.at[core, zb]
        spread.append(send(blk, blk, n5s.at[0], n5r.at[0], sib))
        for i, dz in enumerate(NEAR):
            spread.append(send(blk, blk, n5s.at[1 + i], n5r.at[1 + i], at_z(dz, core)))
            spread.append(send(blk, blk, n5s.at[4 + i], n5r.at[4 + i], at_z(dz, other)))
        c_din.wait()
        drow = jnp.broadcast_to(
            din[:, pl.ds(pl.multiple_of(tp * cols, cols), cols)].astype(F32), (16, cols)
        ).astype(BF16)
        for c in spread:
            c.wait_recv()
        new_down = nb[0].reshape(rank, cols)
        new_up = nb[1].reshape(rank, cols)
        outs = [
            pltpu.make_async_copy(nb.at[0], ndown, oc.at[0]),
            pltpu.make_async_copy(nb.at[1], nup, oc.at[1]),
        ]
        for c in outs:
            c.start()

    with jax.named_scope("decode_hidden"):
        hid = lax.dot_general(drow, new_down, NT, preferred_element_type=F32)[:1]
        scale_part = part[:1, cols:cols + 2 * rank]
        scale_part = scale_part + pltpu.roll(scale_part, rank, 1)
        dh[tp] = jnp.concatenate([hid, scale_part[:, :rank]], axis=1)
        hid_c = []
        for d in range(1, tps):
            hid_c.append(send(dh.at[tp], dh.at[tp], dhs.at[d - 1], dhr.at[d - 1], (role, grp, (tp + d) % tps)))
        for c in hid_c:
            c.wait_recv()
        both = jnp.sum(dh[...], axis=0)
        scale_total = pltpu.roll(both, rank, 1)[:, :rank]
        new_scales = ls_row - (rate_scale * step_scale) * scale_total
        nscale[...] = new_scales
        dscaled = (both[:, :rank] * (1.0 / math.sqrt(width)) * new_scales)
        dscaled = jnp.broadcast_to(dscaled, (16, rank)).astype(BF16)
        c_bq.wait()
        q = jnp.dot(dscaled, new_up, preferred_element_type=F32)[:1] * (1.0 / math.sqrt(rank))
        q = bq[:, pl.ds(pl.multiple_of(tp * cols, cols), cols)].astype(F32) + q
        mine_n = cols // HD
        q = jnp.concatenate([q[:, h * HD:(h + 1) * HD] for h in range(mine_n)] + [jnp.zeros((16 - mine_n, HD), F32)], axis=0).astype(BF16)

    with jax.named_scope("attend"):
        c_fk.wait()
        c_fv.wait()
        for c in caches:
            c.wait_recv()
        hs = pl.ds(pl.multiple_of(head * HD, HD), HD)
        n_pos = tps * kv.shape[2]
        keys = kv[0].reshape(n_pos, HD)
        values = kv[1].reshape(n_pos, HD)
        key_scale = 1.0 / math.sqrt(HD)
        s = lax.dot_general(q, keys, NT, preferred_element_type=F32) * key_scale
        fresh = jnp.sum(q.astype(F32) * fk[:, hs].astype(F32), axis=1, keepdims=True) * key_scale
        live = lax.broadcasted_iota(jnp.int32, s.shape, 1) < lengths[0]
        high = jnp.maximum(jnp.max(jnp.where(live, s, -1e30), axis=1, keepdims=True), fresh)
        w = jnp.where(live, jnp.exp(s - high), 0.0)
        fw = jnp.exp(fresh - high)
        den = jnp.sum(w, axis=1, keepdims=True) + fw
        num = jnp.dot(w.astype(BF16), values, preferred_element_type=F32)
        num = num + fw.astype(BF16).astype(F32) * fv[:, hs].astype(F32)
        res = num / den
        atb[tp] = res[:mine_n]

    with jax.named_scope("spread_attended"):
        at_c = []
        for d in range(1, tps):
            at_c.append(send(atb.at[tp], atb.at[tp], ats.at[d - 1], atr.at[d - 1], (role, grp, (tp + d) % tps)))
        for c in at_c:
            c.wait_recv()
        for i in range(tps):
            rows = atb[i].astype(BF16)
            for h in range(mine_n):
                at = (i * mine_n + h) * HD
                att[:, at:at + HD] = rows[h:h + 1, :]

    with jax.named_scope("drain"):
        c_xs.wait_send()
        for c in sends:
            c.wait_send()
        for c in outs:
            c.wait()


def place(*refs):
    n = len(refs) // 2
    copies = [pltpu.make_async_copy(refs[i], refs[n + i], refs[-1].at[i]) for i in range(n)]
    for c in copies:
        c.start()
    for c in copies:
        c.wait()


def body(*args):
    learn, grad, fdown = args[0], args[1], args[2]
    roles, grps, tps = (lax.axis_size(a) for a in ("role", "grp", "tp"))
    rank, cols = fdown.shape
    toks, width = learn.shape
    local_pos = args[8].shape[1]
    n_far = grps // 2 // ZL - 1
    n_team = roles * ZL - 1
    mine_n = cols // HD
    kvw = args[10].shape[1]
    half, quart, rb = rank // 2, rank // 4, rank // ZL
    args = list(args)
    args[4] = args[4].T
    hbm = pl.BlockSpec(memory_space=pltpu.HBM)
    smem = pl.BlockSpec(memory_space=pltpu.SMEM)
    vmem = pl.BlockSpec(memory_space=pltpu.VMEM)
    in_specs = [hbm] * 5 + [smem] + [hbm] * 6 + [smem]
    dma = pltpu.SemaphoreType.DMA
    outs = pl.pallas_call(
        lambda *refs: kernel(roles, grps, tps, *refs),
        out_shape=(
            jax.ShapeDtypeStruct((ZL, rb, cols), BF16),
            jax.ShapeDtypeStruct((ZL, rb, cols), BF16),
            jax.ShapeDtypeStruct((1, rank), F32),
            jax.ShapeDtypeStruct((1, HEADS * HD), BF16),
        ),
        in_specs=in_specs,
        out_specs=(hbm, hbm, vmem, vmem),
        scratch_shapes=[
            pltpu.VMEM((2, toks, width), BF16),
            pltpu.VMEM((NX, NY, rank, cols), BF16),
            pltpu.VMEM((2, rank, 2 * toks), F32),
            pltpu.VMEM((NX, NY, rank, cols), BF16),
            pltpu.VMEM((NX - 1, NY, half, cols), BF16),
            pltpu.VMEM((NY - 1, NX, half, cols), BF16),
            pltpu.VMEM((6, half, cols), BF16),
            pltpu.VMEM((3, half, cols), BF16),
            pltpu.VMEM((3, half, cols), BF16),
            pltpu.VMEM((ZL, rb, cols + 2 * rank), BF16),
            pltpu.VMEM((n_team, rb, cols + 2 * rank), BF16),
            pltpu.VMEM((rb, cols + 2 * rank), BF16),
            pltpu.VMEM((n_far, rb, cols + 2 * rank), BF16),
            pltpu.VMEM((2, ZL, rb, cols), BF16),
            pltpu.VMEM((tps, 1, 2 * rank), F32),
            pltpu.VMEM((2, local_pos, kvw), BF16),
            pltpu.VMEM((2, tps, local_pos, HD), BF16),
            pltpu.VMEM((tps, mine_n, HD), F32),
            pltpu.VMEM(args[4].shape, F32),
            pltpu.VMEM((1, width), BF16),
            pltpu.VMEM((1, width), BF16),
            pltpu.VMEM((1, kvw), BF16),
            pltpu.VMEM((1, kvw), BF16),
            dma((9,)),
            dma((1,)), dma((1,)),
            dma((7,)), dma((7,)),
            dma((21,)), dma((21,)),
            dma((1,)), dma((1,)),
            dma((28,)), dma((28,)),
            dma((7,)), dma((7,)),
            dma((2 * tps - 2,)), dma((2 * tps - 2,)),
            dma((n_team,)), dma((n_team,)),
            dma((n_far,)), dma((n_far,)),
            dma((7,)), dma((7,)),
            dma((tps - 1,)), dma((tps - 1,)),
            dma((tps - 1,)), dma((tps - 1,)),
            dma((2,)),
        ],
        compiler_params=pltpu.CompilerParams(
            collective_id=0, has_side_effects=True, vmem_limit_bytes=60 * 1024 * 1024
        ),
    )(*args)
    results = (outs[0].reshape(rank, cols), outs[1].reshape(rank, cols), outs[2], outs[3])
    n = len(results)
    results = pl.pallas_call(
        place,
        out_shape=tuple(jax.ShapeDtypeStruct(r.shape, r.dtype) for r in results),
        in_specs=[hbm] * n,
        out_specs=(vmem,) * n,
        scratch_shapes=[dma((n,))],
    )(*results)
    return (results[0], results[1], results[2].reshape(rank), results[3])


def solution(mesh):
    in_specs = (
        P(("role", "grp", "tp"), None),
        P(("role", "grp", "tp"), None),
        P(None, "tp"),
        P(None, "tp"),
        P(),
        P(),
        P(("role", "grp"), None),
        P(("role", "grp"), None),
        P(("role", "grp"), "tp", None),
        P(("role", "grp"), "tp", None),
        P(("role", "grp"), None),
        P(("role", "grp"), None),
        P(("role", "grp")),
    )
    out_specs = (P(None, "tp"), P(None, "tp"), P(), P(("role", "grp"), None))
    return jax.shard_map(body, mesh=mesh, in_specs=in_specs, out_specs=out_specs, check_vma=False)
```
